32 devices in a mesh: dp: 2 (over x), seq: 16 (over z, y, core).
Axes of the slice: x: 2, y: 2, z: 4, core: 2. Of those that a mesh axis runs over, the one named last changes fastest.
Arguments:
- hidden: bfloat16 [2, 2048, 1024], P('dp', 'seq'), may hold values from -6 to 6
- letters: int32 [2, 2048], P('dp', 'seq'), may hold values from 0 to 3
- gate_input: bfloat16 [2, 2048, 1024], P('dp', 'seq'), may hold values from -6 to 6
- cotangent: bfloat16 [2, 2048, 1024], P('dp', 'seq'), may hold values from -6 to 6
- embedding: float32 [4, 1024], replicated, may hold values from -6 to 6
- filter_taps: bfloat16 [4, 128, 1024], P(None, 'seq'), may hold values from -0.25 to 0.25
Outputs:
- output: bfloat16 [2, 2048, 1024], P('dp', 'seq')
- hidden_grad: bfloat16 [2, 2048, 1024], P('dp', 'seq')
- gate_grad: bfloat16 [2, 2048, 1024], P('dp', 'seq')
- filter_grad: float32 [4, 128, 1024], P(None, 'seq')
- embedding_grad: float32 [4, 1024], replicated
The draws below stay inside these ranges and needn't reach their ends.
All inputs are finite; a program needn't handle non-finite values.
Results may differ from the reference program's by a relative error of at most 0.0049.
Values may be sent and summed in bfloat16 or wider, within the bound.
No kernel may reach another device: no remote copies, remote signals or barrier semaphores. Data moves between devices by JAX's collectives and lax.ppermute only.
A program may use at most 128 MiB of HBM per device.

```python
import jax
import jax.numpy as jnp
from jax import lax

CHANNELS = 1024
STRETCH = 128
REACH = 4
LETTERS = 4
TAPS = 512
BATCH = 2
LENGTH = 2048


def plant(values, stream_key, low, high):
    dims = values.shape
    place = [jax.random.randint(jax.random.fold_in(stream_key, axis), (), 0, dims[axis]) for axis in range(len(dims))]
    values = values.at[tuple(place)].set(low)
    longest = dims.index(max(dims))
    place[longest] = (place[longest] + 1) % dims[longest]
    return values.at[tuple(place)].set(high)


def block_scale(rng, shape, pieces, least, largest):
    loudness, own = 1.0, jax.random.fold_in(rng, 6)
    for position, parts in pieces:
        heights = jnp.exp(jax.random.uniform(jax.random.fold_in(own, position), (parts,), jnp.float32, least / len(pieces), largest / len(pieces)))
        loudness = loudness * jnp.repeat(heights, shape[position] // parts).reshape([-1 if axis == position else 1 for axis in range(len(shape))])
    return loudness


def bell_draw(rng, dims, deviation, reach, shards=(), dtype=jnp.bfloat16):
    array = deviation * jax.random.normal(rng, dims, jnp.float32)
    if shards:
        array = array * block_scale(rng, dims, shards, -0.22, 0.18)
    return jnp.clip(array, -reach, reach).astype(dtype)


def setup_inputs(seed: int = 0) -> dict:
    splits = jax.random.split(jax.random.key(seed), 7)
    hidden = bell_draw(splits[0], (BATCH, LENGTH, CHANNELS), 1.0, 6.0, ((0, 2), (1, 16)))
    letters = plant(jax.random.randint(splits[1], (BATCH, LENGTH), 0, 4), jax.random.fold_in(splits[1], 1), 0, 3).astype(jnp.int32)
    gate_input = bell_draw(splits[2], (BATCH, LENGTH, CHANNELS), 1.0, 6.0, ((0, 2), (1, 16)))
    cotangent = bell_draw(splits[3], (BATCH, LENGTH, CHANNELS), 1.0, 6.0, ((0, 2), (1, 16)))
    embedding = bell_draw(splits[4], (LETTERS, CHANNELS), 1.0, 6.0, (), jnp.float32)
    filter_taps = bell_draw(splits[5], (REACH, STRETCH, CHANNELS), TAPS ** -0.5, 0.25, ((1, 16),))
    return {"hidden": hidden, "letters": letters, "gate_input": gate_input, "cotangent": cotangent, "embedding": embedding, "filter_taps": filter_taps}


def causal_sum(signal, kernel):
    extent = signal.shape[0] + kernel.shape[0]
    spectrum = jnp.fft.rfft(signal, extent, axis=0) * jnp.fft.rfft(kernel, extent, axis=0)
    return jnp.fft.irfft(spectrum, extent, axis=0)[: signal.shape[0]]


def ahead_sum(signal, kernel):
    return jnp.flip(causal_sum(jnp.flip(signal, axis=0), kernel), axis=0)


def lag_sums(leading, earlier, lag_count):
    extent = leading.shape[0] + lag_count
    spectrum = jnp.fft.rfft(leading, extent, axis=0) * jnp.conj(jnp.fft.rfft(earlier, extent, axis=0))
    return jnp.fft.irfft(spectrum, extent, axis=0)[:lag_count]


def reference(hidden, letters, gate_input, cotangent, embedding, filter_taps):
    kernel = filter_taps.astype(jnp.float32).reshape(TAPS, CHANNELS)
    mirrored = jnp.flip(kernel, axis=1)
    norming = (BATCH * LENGTH) ** -0.5

    def one_sequence(operands):
        row_block, letter_row, gating, upstream = operands
        onehot = (letter_row[:, None] == jnp.arange(LETTERS).astype(jnp.int32)[None, :]).astype(jnp.float32)
        mixed = row_block.astype(jnp.float32) + jnp.dot(onehot, embedding, precision=lax.Precision.HIGHEST)
        values_wide = lax.optimization_barrier(mixed.astype(jnp.bfloat16)).astype(jnp.float32)
        forward_field = causal_sum(values_wide, kernel) + ahead_sum(values_wide, mirrored)
        gating_wide = gating.astype(jnp.float32)
        upstream_wide = upstream.astype(jnp.float32)
        output = (gating_wide * forward_field).astype(jnp.bfloat16)
        gate_grad = (upstream_wide * forward_field).astype(jnp.bfloat16)
        field_grad = lax.optimization_barrier((upstream_wide * gating_wide).astype(jnp.bfloat16)).astype(jnp.float32)
        values_grad = ahead_sum(field_grad, kernel) + causal_sum(field_grad, mirrored)
        hidden_grad = values_grad.astype(jnp.bfloat16)
        taps_term = lag_sums(field_grad, values_wide, TAPS) + lag_sums(jnp.flip(values_wide, axis=1), jnp.flip(field_grad, axis=1), TAPS)
        letter_term = jnp.dot(onehot.T, values_grad, precision=lax.Precision.HIGHEST)
        return output, hidden_grad, gate_grad, taps_term, letter_term

    results = lax.map(one_sequence, (hidden, letters, gate_input, cotangent))
    filter_grad = (jnp.sum(results[3], axis=0) * norming).reshape(REACH, STRETCH, CHANNELS)
    embedding_grad = jnp.sum(results[4], axis=0) * norming
    return results[0], results[1], results[2], filter_grad, embedding_grad
```

```python
import math

import jax
import jax.numpy as jnp
import numpy as np
from jax import lax
from jax.experimental import pallas as pl
from jax.experimental.pallas import tpu as pltpu
from jax.sharding import PartitionSpec as P

BLOCK = 512
COLS = 256
LANES = 128
STEP = 16

F32 = jnp.float32
BF16 = jnp.bfloat16


def tables():
    frequency = np.arange(BLOCK)[:, None]
    moment = np.arange(BLOCK)[None, :]
    angles = (frequency * moment % (2 * BLOCK)) * (2.0 * np.pi / (2 * BLOCK))
    sines = -np.sin(angles)
    sines[0] = 1.0 - 2.0 * (np.arange(BLOCK) % 2)
    forward = np.concatenate([np.cos(angles), sines], axis=0)
    weights = np.full((2 * BLOCK, 1), 1.0 / BLOCK)
    weights[0] = weights[BLOCK] = 0.5 / BLOCK
    backward = (forward * weights).T

    def halves(table):
        high = table.astype(jnp.bfloat16)
        return high, (table - high.astype(np.float64)).astype(jnp.bfloat16)

    return (*halves(forward), *halves(backward))


def iota(shape, axis):
    return lax.broadcasted_iota(jnp.int32, shape, axis)


def matmul(left, right):
    return jnp.dot(left, right, preferred_element_type=F32)


def swap_matrix():
    row, lane = iota((512, 512), 0), iota((1, 512), 1)
    source = ((lane >> 5) & 3) * 128 + (lane >> 7) * 32 + (lane & 31)
    return jnp.where(row == source, 1.0, 0.0).astype(BF16)


def channel_source(lane):
    group, spot = lane >> 5, lane & 31
    return jnp.where(spot < 16, 16 * group + spot, 271 - 16 * group - spot)


def gather_channels():
    row, lane = iota((256, 256), 0), iota((1, 256), 1)
    return jnp.where(row == channel_source(lane), 1.0, 0.0).astype(BF16)


def return_channels():
    row, lane = iota((256, 1), 0), iota((256, 256), 1)
    return jnp.where(channel_source(row) == lane, 1.0, 0.0).astype(BF16)


def pack_kernel(hidden_ref, letters_ref, gate_ref, upstream_ref, embedding_ref, taps_ref, send_ref):
    letters = letters_ref[...]
    square = iota((128, 128), 0) == iota((128, 128), 1)
    letter = jnp.sum(jnp.where(square, letters.astype(F32), 0.0), axis=1, keepdims=True)
    added = embedding_ref[0:1, :]
    for index in range(1, 4):
        added = jnp.where(letter == float(index), embedding_ref[index : index + 1, :], added)
    values = (hidden_ref[0].astype(F32) + added).astype(BF16)
    field_grad = (upstream_ref[0].astype(F32) * gate_ref[0].astype(F32)).astype(BF16)
    taps = taps_ref[pl.ds(2 * lax.axis_index("dp"), 2)].astype(F32).reshape(16, 1024).astype(BF16)
    gather = gather_channels()
    swap = swap_matrix()
    rows = []
    for part in (values, field_grad, taps):
        for u in range(4):
            pair = jnp.concatenate(
                [part[:, 128 * u : 128 * u + 128], part[:, 896 - 128 * u : 1024 - 128 * u]], axis=1
            )
            rows.append(matmul(pair, gather).astype(BF16))
    stacked = []
    for part in range(2):
        for m in range(8):
            block = rows[4 * part + m // 2][:, 128 * (m % 2) : 128 * (m % 2) + 128]
            stacked.append(jnp.concatenate([block[32 * q : 32 * q + 32] for q in range(4)], axis=1))
    moved = matmul(jnp.concatenate(stacked, axis=0), swap).astype(BF16)
    for part in range(2):
        for m in range(8):
            for d in range(4):
                start = 256 * part + 32 * m
                send_ref[4 * m + d, 32 * part : 32 * part + 32, :] = moved[
                    start : start + 32, 128 * d : 128 * d + 128
                ]
    stacked = []
    for m in range(8):
        block = rows[8 + m // 2][:, 128 * (m % 2) : 128 * (m % 2) + 128].astype(F32)
        stacked.append(jnp.concatenate([block[0:8], block[8:16]], axis=1))
    row, lane = iota((256, 512), 0), iota((1, 512), 1)
    spot = lane & 127
    source = jnp.where(spot < 64, (spot >> 5) * 128 + (lane >> 7) * 32 + (spot & 31), -1)
    spread = jnp.where(row == source, 1.0, 0.0).astype(BF16)
    moved = matmul(jnp.concatenate(stacked, axis=0).astype(BF16), spread)
    line = jnp.broadcast_to(letters.astype(F32), (8, 128))
    which, lane = iota((8, 128), 0), iota((8, 128), 1)
    shown = jnp.where(which == 0, pltpu.roll(line, 64, 1), jnp.where(which == 1, line, 0.0))
    shown = jnp.where(lane >= 64, shown, 0.0)
    for m in range(8):
        for d in range(4):
            piece = moved[8 * m : 8 * m + 8, 128 * d : 128 * d + 128] + shown
            send_ref[4 * m + d, 64:72, :] = piece.astype(BF16)


def spectra_step(spectra_ref, high_ref, low_ref, narrow, width, base, first):
    top, under = pl.ds(base, STEP), pl.ds(BLOCK + base, STEP)

    def load(start, size):
        return spectra_ref[top, start : start + size], spectra_ref[under, start : start + size]

    def twice(pair):
        return tuple(jnp.concatenate([part, part], axis=1) for part in pair)

    values, grads = load(0, COLS), load(COLS, COLS)
    own, mirror = twice(load(2 * COLS, LANES)), twice(load(2 * COLS + LANES, LANES))
    lane = iota((STEP, COLS), 1)
    sign = (1 - 2 * (iota((STEP, COLS), 0) & 1)).astype(F32)
    before_sign = jnp.where(lane >= width, sign, 0.0)
    after_sign = jnp.where(lane < COLS - width, sign, 0.0)
    real_row = iota((STEP, COLS), 0) == 0

    def with_earlier(pair):
        return tuple(part + before_sign * pltpu.roll(part, width, 1) for part in pair)

    def with_later(pair):
        return tuple(part + after_sign * pltpu.roll(part, COLS - width, 1) for part in pair)

    def settle(a, b, real, imaginary):
        if first:
            real = jnp.where(real_row, a[0] * b[0], real)
            imaginary = jnp.where(real_row, a[1] * b[1], imaginary)
        return real, imaginary

    def times(a, b):
        return settle(a, b, a[0] * b[0] - a[1] * b[1], a[0] * b[1] + a[1] * b[0])

    def times_conjugate(a, b):
        return settle(a, b, a[0] * b[0] + a[1] * b[1], a[1] * b[0] - a[0] * b[1])

    def plus(a, b):
        return a[0] + b[0], a[1] + b[1]

    def column_sum(pair):
        total = tuple(part[:, :LANES] + part[:, LANES:] for part in pair)
        shift = LANES // 2
        while shift >= narrow:
            total = tuple(part + pltpu.roll(part, shift, 1) for part in total)
            shift //= 2
        return total

    values_back, values_on = with_earlier(values), with_later(values)
    grads_back, grads_on = with_earlier(grads), with_later(grads)
    field = plus(times(values_back, own), times_conjugate(values_on, mirror))
    back = plus(times(grads_back, mirror), times_conjugate(grads_on, own))
    causal = column_sum(times_conjugate(grads, values_back))
    ahead = column_sum(times_conjugate(values_on, grads))
    lags = plus(causal, tuple(pltpu.roll(part, narrow // 2, 1) for part in ahead))
    for rows, part in ((top, 0), (under, 1)):
        for start, size, pair in ((0, COLS, field), (COLS, COLS, back), (2 * COLS, LANES, lags)):
            high = pair[part].astype(BF16)
            high_ref[rows, start : start + size] = high
            low_ref[rows, start : start + size] = (pair[part] - high.astype(F32)).astype(BF16)


def transforms(samples_ref, table_refs, spectra_ref, high_ref, low_ref, result_ref, narrow, width):
    forward_high, forward_low, backward_high, backward_low = table_refs
    for part in range(4):
        rows = slice(256 * part, 256 * part + 256)
        spectra_ref[rows, :] = matmul(forward_high[rows, :], samples_ref[...]) + matmul(
            forward_low[rows, :], samples_ref[...]
        )
    step = lambda base, first: spectra_step(
        spectra_ref, high_ref, low_ref, narrow, width, base, first
    )
    step(0, True)

    def body(index, carry):
        step(pl.multiple_of(index * STEP, STEP), False)
        return carry

    lax.fori_loop(1, BLOCK // STEP, body, 0)
    for part in range(2):
        rows = slice(256 * part, 256 * part + 256)
        result_ref[rows, :] = (
            matmul(backward_high[rows, :], high_ref[...])
            + matmul(backward_low[rows, :], high_ref[...])
            + matmul(backward_high[rows, :], low_ref[...])
        )


def letter_sums(values_grad, choice, belongs, narrow):
    high = values_grad.astype(BF16)
    low = (values_grad - high.astype(F32)).astype(BF16)
    sums = jnp.where(belongs, matmul(choice, high) + matmul(choice, low), 0.0)
    groups = sums.shape[0] // 4
    rows = [jnp.sum(sums[groups * a : groups * a + groups], axis=0, keepdims=True) for a in range(4)]
    total = jnp.concatenate(rows, axis=0)
    total = total[:, :LANES] + total[:, LANES:]
    shift = LANES // 2
    while shift >= narrow:
        total = total + pltpu.roll(total, shift, 1)
        shift //= 2
    return total


WORK = [
    pltpu.VMEM((BLOCK, 3 * COLS), BF16),
    pltpu.VMEM((2 * BLOCK, 3 * COLS), F32),
    pltpu.VMEM((2 * BLOCK, 2 * COLS + LANES), BF16),
    pltpu.VMEM((2 * BLOCK, 2 * COLS + LANES), BF16),
    pltpu.VMEM((BLOCK, 2 * COLS + LANES), F32),
]


def middle_kernel(
    norming, receive_ref, fh_ref, fl_ref, bh_ref, bl_ref, send_ref,
    samples_ref, spectra_ref, high_ref, low_ref, result_ref,
):
    swap = swap_matrix()
    places = [(part, u, s) for part in range(2) for u in range(2) for s in range(4)]
    stacked = []
    for part, u, s in places:
        pieces = [
            receive_ref[16 * d + 4 * (2 * u + j) + s, 32 * part : 32 * part + 32, :]
            for j in range(2)
            for d in range(2)
        ]
        stacked.append(jnp.concatenate(pieces, axis=1))
    moved = matmul(jnp.concatenate(stacked, axis=0), swap).astype(BF16)
    for index, (part, u, s) in enumerate(places):
        for q in range(4):
            start = 128 * s + 32 * q
            samples_ref[start : start + 32, 256 * part + 128 * u : 256 * part + 128 * u + 128] = moved[
                32 * index : 32 * index + 32, 128 * q : 128 * q + 128
            ]
    tails = receive_ref[:, 64:72, :].astype(F32)
    row, lane = iota((128, 256), 0), iota((1, 256), 1)
    spot = (lane & 31) ^ ((lane >> 7) << 4)
    for d in range(2):
        tail = tails[16 * d : 16 * d + 16].reshape(128, 128).astype(BF16)
        for k in range(2):
            spread = jnp.where(row == 32 * k + spot, 1.0, 0.0).astype(BF16)
            start = 128 * (2 * d + k)
            samples_ref[start : start + 128, 512:768] = matmul(tail, spread).astype(BF16)
    transforms(
        samples_ref, (fh_ref, fl_ref, bh_ref, bl_ref), spectra_ref, high_ref, low_ref, result_ref, 32, 64
    )
    field_pieces = []
    for part, u, s in places:
        pieces = [
            result_ref[128 * s + 32 * q : 128 * s + 32 * q + 32, 256 * part + 128 * u : 256 * part + 128 * u + 128]
            for q in range(4)
        ]
        field_pieces.append(jnp.concatenate(pieces, axis=1).astype(BF16))
    moved = matmul(jnp.concatenate(field_pieces, axis=0), swap).astype(BF16)
    for index, (part, u, s) in enumerate(places):
        for j in range(2):
            for d in range(2):
                group = 2 * j + d
                send_ref[16 * d + 4 * (2 * u + j) + s, 32 * part : 32 * part + 32, :] = moved[
                    32 * index : 32 * index + 32, 128 * group : 128 * group + 128
                ]
    quarter = iota((128, 128), 1) >> 5
    lags = result_ref[0:128, 512:640]
    for k in range(1, 4):
        lags = jnp.where(quarter == k, result_ref[128 * k : 128 * k + 128, 512:640], lags)
    lags = (lags * norming).reshape(16, 8, 128).astype(BF16)
    send_ref[0:16, 64:72, :] = lags
    send_ref[16:32, 64:72, :] = lags
    line = iota((32, 128), 1)
    letters = jnp.where(line < 64, pltpu.roll(tails[:, 0, :], 64, 1), tails[:, 1, :])
    source = iota((32, 128), 0)
    choice = []
    for a in range(4):
        chosen = jnp.where(letters == float(a), 1.0, 0.0)
        choice.append(
            jnp.concatenate([jnp.where((source & 3) == s, chosen, 0.0) for s in range(4)], axis=1)
        )
    choice = jnp.concatenate(choice, axis=0).astype(BF16)
    source = iota((128, 256), 0) & 31
    belongs = (((source >> 2) & 3) * 2 + (source >> 4)) == (iota((128, 256), 1) >> 5)
    sums = letter_sums(result_ref[:, 256:512], choice, belongs, 32) * norming
    high = sums.astype(BF16).astype(F32)
    tile = jnp.concatenate([high, sums - high], axis=0).astype(BF16)
    for index in range(32):
        send_ref[index, 72:80, :] = tile


def finish_kernel(receive_ref, gate_ref, upstream_ref, out_ref, hidden_ref, gated_ref, filter_ref, embedding_ref):
    swap = swap_matrix()
    back = return_channels()
    stacked = []
    for part in range(2):
        for m in range(8):
            pieces = [receive_ref[4 * m + d, 32 * part : 32 * part + 32, :] for d in range(4)]
            stacked.append(jnp.concatenate(pieces, axis=1))
    moved = matmul(jnp.concatenate(stacked, axis=0), swap).astype(BF16)
    for u in range(4):
        halves = []
        for part in range(2):
            columns = []
            for m in (2 * u, 2 * u + 1):
                start = 256 * part + 32 * m
                columns.append(
                    jnp.concatenate(
                        [moved[start : start + 32, 128 * q : 128 * q + 128] for q in range(4)], axis=0
                    )
                )
            halves.append(matmul(jnp.concatenate(columns, axis=1), back))
        for start, lane in ((128 * u, 0), (896 - 128 * u, 128)):
            there = slice(start, start + 128)
            field = halves[0][:, lane : lane + 128]
            out_ref[0, :, there] = (gate_ref[0, :, there].astype(F32) * field).astype(BF16)
            gated_ref[0, :, there] = (upstream_ref[0, :, there].astype(F32) * field).astype(BF16)
            hidden_ref[0, :, there] = halves[1][:, lane : lane + 128].astype(BF16)
    tails = receive_ref[:, 64:80, :].astype(F32)
    stacked = [
        jnp.concatenate([tails[4 * m + d, 0:8, :] for d in range(4)], axis=1) for m in range(8)
    ]
    moved = matmul(jnp.concatenate(stacked, axis=0).astype(BF16), swap)
    quarter = iota((8, 128), 1) >> 5
    for u in range(4):
        columns = []
        for m in (2 * u, 2 * u + 1):
            rows = [moved[8 * m : 8 * m + 8, 128 * k : 128 * k + 128] for k in range(4)]
            sums = tails[4 * m, 8:16, :]
            for d in range(1, 4):
                sums = jnp.where(quarter == d, tails[4 * m + d, 8:16, :], sums)
            columns.append(jnp.concatenate(rows + [sums], axis=0))
        done = matmul(jnp.concatenate(columns, axis=1).astype(BF16), back)
        for start, lane in ((128 * u, 0), (896 - 128 * u, 128)):
            there = slice(start, start + 128)
            filter_ref[:, :, there] = done[0:32, lane : lane + 128].reshape(4, 8, 128)
            embedding_ref[:, there] = done[32:36, lane : lane + 128] + done[36:40, lane : lane + 128]


def call(kernel, shapes, scratch=()):
    return pl.pallas_call(
        kernel,
        out_shape=shapes,
        scratch_shapes=scratch,
        compiler_params=pltpu.CompilerParams(vmem_limit_bytes=48 * 1024 * 1024),
    )


def packed_device(hidden, letters, gate_input, cotangent, embedding, filter_taps, norming):
    send = call(pack_kernel, jax.ShapeDtypeStruct((32, 72, 128), BF16))(
        hidden, letters, gate_input, cotangent, embedding, filter_taps
    )
    received = lax.all_to_all(send, ("dp", "seq"), 0, 0, tiled=True)

    def middle(*refs):
        middle_kernel(norming, *refs)

    send = call(middle, jax.ShapeDtypeStruct((32, 80, 128), BF16), WORK)(received, *tables())
    received = lax.all_to_all(send, ("dp", "seq"), 0, 0, tiled=True)
    shape = jax.ShapeDtypeStruct(hidden.shape, BF16)
    output, hidden_grad, gate_grad, filter_grad, embedding_grad = call(
        finish_kernel,
        (
            shape,
            shape,
            shape,
            jax.ShapeDtypeStruct(filter_taps.shape, F32),
            jax.ShapeDtypeStruct(embedding.shape, F32),
        ),
    )(received, gate_input, cotangent)
    return output, hidden_grad, gate_grad, filter_grad, embedding_grad


def plain_kernel(
    narrow, width, samples_ref, letters_ref, fh_ref, fl_ref, bh_ref, bl_ref,
    field_ref, back_ref, lags_ref, sums_ref, spectra_ref, high_ref, low_ref, result_ref,
):
    transforms(
        samples_ref, (fh_ref, fl_ref, bh_ref, bl_ref), spectra_ref, high_ref, low_ref, result_ref, narrow, width
    )
    field_ref[...] = result_ref[:, 0:256].astype(BF16)
    back_ref[...] = result_ref[:, 256:512].astype(BF16)
    lags_ref[...] = result_ref[:, 512:640]
    letters = letters_ref[...]
    groups = COLS // narrow
    choice = jnp.concatenate(
        [jnp.where(letters == float(a), 1.0, 0.0) for a in range(4)], axis=0
    ).astype(BF16)
    shape = (4 * groups, COLS)
    belongs = (iota(shape, 0) & (groups - 1)) == iota(shape, 1) // narrow
    sums_ref[...] = letter_sums(result_ref[:, 256:512], choice, belongs, narrow)


def plain_device(hidden, letters, gate_input, cotangent, embedding, filter_taps, norming):
    axes = ("dp", "seq")
    copies, stretches = lax.axis_size("dp"), lax.axis_size("seq")
    devices = copies * stretches
    stretch, channels = hidden.shape[1], hidden.shape[2]
    narrow = channels // devices
    half = narrow // 2
    blocks = stretch * stretches // BLOCK
    low = np.arange(channels // 2).reshape(devices, half)
    order = np.concatenate([low, channels - 1 - low], axis=1).reshape(-1)
    restore = np.argsort(order)
    onehot = (letters[0][:, None] == jnp.arange(embedding.shape[0], dtype=jnp.int32)[None, :]).astype(F32)
    added = jnp.dot(onehot, embedding, precision=lax.Precision.HIGHEST)
    values = (hidden[0].astype(F32) + added).astype(BF16)
    gate_wide, upstream = gate_input[0].astype(F32), cotangent[0].astype(F32)
    field_grad = (upstream * gate_wide).astype(BF16)

    def scatter(array):
        parts = jnp.take(array, order, axis=1).reshape(stretch, devices, narrow).swapaxes(0, 1)
        parts = lax.all_to_all(parts, axes, 0, 0, tiled=True)
        parts = parts.reshape(copies, blocks, BLOCK, narrow)
        return parts.transpose(2, 1, 0, 3).reshape(BLOCK, COLS)

    def gather(columns):
        parts = columns.reshape(BLOCK, blocks, copies, narrow).transpose(2, 1, 0, 3)
        parts = parts.reshape(devices, stretch, narrow)
        parts = lax.all_to_all(parts, axes, 0, 0, tiled=True)
        return jnp.take(parts.swapaxes(0, 1).reshape(stretch, channels), restore, axis=1)

    taps = lax.all_gather(filter_taps, "seq", axis=1, tiled=True).reshape(BLOCK, channels)
    mine = lax.axis_index("dp") * stretches + lax.axis_index("seq")
    own = lax.dynamic_slice_in_dim(jnp.take(taps, order, axis=1), mine * narrow, narrow, axis=1)
    mirror = jnp.roll(own, half, axis=1)
    repeats = LANES // narrow
    samples = jnp.concatenate(
        [scatter(values), scatter(field_grad), jnp.tile(own, (1, repeats)), jnp.tile(mirror, (1, repeats))], axis=1
    )
    marks = lax.all_gather(letters[0].astype(F32), axes, tiled=True)
    marks = marks.reshape(copies, blocks, BLOCK).swapaxes(0, 1).reshape(copies * blocks, BLOCK)

    def kernel(*refs):
        plain_kernel(narrow, copies * narrow, *refs)

    field, back, lags, sums = call(
        kernel,
        (
            jax.ShapeDtypeStruct((BLOCK, COLS), BF16),
            jax.ShapeDtypeStruct((BLOCK, COLS), BF16),
            jax.ShapeDtypeStruct((BLOCK, LANES), F32),
            jax.ShapeDtypeStruct((embedding.shape[0], LANES), F32),
        ),
        WORK[1:],
    )(samples, marks, *tables())
    small = jnp.concatenate([lags[:, :narrow], sums[:, :narrow]], axis=0) * norming
    small = jnp.take(lax.all_gather(small, axes, axis=1, tiled=True), restore, axis=1)
    rows = filter_taps.shape[1]
    filter_grad = lax.dynamic_slice_in_dim(
        small[:BLOCK].reshape(filter_taps.shape[0], stretch, channels), lax.axis_index("seq") * rows, rows, axis=1
    )
    field_rows, grad_rows = gather(field).astype(F32), gather(back)
    output = (gate_wide * field_rows).astype(BF16)[None]
    gate_grad = (upstream * field_rows).astype(BF16)[None]
    return output, grad_rows[None], gate_grad, filter_grad, small[BLOCK:]


def per_device(hidden, letters, gate_input, cotangent, embedding, filter_taps):
    copies, stretches = lax.axis_size("dp"), lax.axis_size("seq")
    norming = 1.0 / math.sqrt(copies * hidden.shape[0] * hidden.shape[1] * stretches)
    device = packed_device if (copies, stretches) == (2, 16) else plain_device
    return device(hidden, letters, gate_input, cotangent, embedding, filter_taps, norming)


def solution(mesh):
    return jax.shard_map(
        per_device,
        mesh=mesh,
        in_specs=(
            P("dp", "seq", None),
            P("dp", "seq"),
            P("dp", "seq", None),
            P("dp", "seq", None),
            P(),
            P(None, "seq", None),
        ),
        out_specs=(
            P("dp", "seq", None),
            P("dp", "seq", None),
            P("dp", "seq", None),
            P(None, "seq", None),
            P(),
        ),
        check_vma=False,
    )
```

```python
import math

import jax
import jax.numpy as jnp
import numpy as np
from jax import lax
from jax.experimental import pallas as pl
from jax.experimental.pallas import tpu as pltpu
from jax.sharding import PartitionSpec as P

BLOCK = 512
COLS = 256
LANES = 128
STEP = 16
CHUNK = 128
GROUP = 2

F32 = jnp.float32
BF16 = jnp.bfloat16


def tables():
    frequency = np.arange(BLOCK)[:, None]
    moment = np.arange(BLOCK)[None, :]
    angles = (frequency * moment % (2 * BLOCK)) * (2.0 * np.pi / (2 * BLOCK))
    sines = -np.sin(angles)
    sines[0] = 1.0 - 2.0 * (np.arange(BLOCK) % 2)
    forward = np.stack([np.cos(angles).reshape(-1, CHUNK, BLOCK), sines.reshape(-1, CHUNK, BLOCK)], axis=1)
    forward = forward.reshape(2 * BLOCK, BLOCK)
    weights = np.full((2 * BLOCK, 1), 1.0 / BLOCK)
    weights[0] = weights[CHUNK] = 0.5 / BLOCK
    backward = (forward * weights).T

    def halves(table):
        high = table.astype(jnp.bfloat16)
        return high, (table - high.astype(np.float64)).astype(jnp.bfloat16)

    return (*halves(forward), *halves(backward))


def iota(shape, axis):
    return lax.broadcasted_iota(jnp.int32, shape, axis)


def matmul(left, right):
    return jnp.dot(left, right, preferred_element_type=F32)


def swap_matrix():
    row, lane = iota((512, 512), 0), iota((1, 512), 1)
    source = ((lane >> 5) & 3) * 128 + (lane >> 7) * 32 + (lane & 31)
    return jnp.where(row == source, 1.0, 0.0).astype(BF16)


def channel_source(lane):
    group, spot = lane >> 5, lane & 31
    return jnp.where(spot < 16, 16 * group + spot, 271 - 16 * group - spot)


def gather_channels():
    row, lane = iota((256, 256), 0), iota((1, 256), 1)
    return jnp.where(row == channel_source(lane), 1.0, 0.0).astype(BF16)


def return_channels():
    row, lane = iota((256, 1), 0), iota((256, 256), 1)
    return jnp.where(channel_source(row) == lane, 1.0, 0.0).astype(BF16)


def copy_in(pairs, sems):
    copies = [pltpu.make_async_copy(source, target, sems.at[index]) for index, (source, target) in enumerate(pairs)]
    for copy in copies:
        copy.start()
    return copies


def gathered_rows(part):
    gather = gather_channels()
    rows = []
    for u in range(4):
        pair = jnp.concatenate([part[:, 128 * u : 128 * u + 128], part[:, 896 - 128 * u : 1024 - 128 * u]], axis=1)
        rows.append(matmul(pair, gather).astype(BF16))
    return rows


def send_stretch(part, send_ref, place):
    rows = gathered_rows(part)
    stacked = []
    for m in range(8):
        block = rows[m // 2][:, 128 * (m % 2) : 128 * (m % 2) + 128]
        stacked.append(jnp.concatenate([block[32 * q : 32 * q + 32] for q in range(4)], axis=1))
    moved = matmul(jnp.concatenate(stacked, axis=0), swap_matrix()).astype(BF16)
    for m in range(8):
        for d in range(4):
            send_ref[4 * m + d, place : place + 32, :] = moved[32 * m : 32 * m + 32, 128 * d : 128 * d + 128]


def pack_kernel(
    hidden_hbm, letters_hbm, gate_hbm, upstream_hbm, embedding_hbm, taps_hbm, send_ref,
    hidden_ref, letters_ref, gate_ref, upstream_ref, embedding_ref, taps_ref, sems,
):
    copies = copy_in(
        [
            (letters_hbm, letters_ref),
            (embedding_hbm, embedding_ref),
            (taps_hbm.at[pl.ds(2 * lax.axis_index("dp"), 2)], taps_ref),
            (hidden_hbm, hidden_ref),
            (gate_hbm, gate_ref),
            (upstream_hbm, upstream_ref),
        ],
        sems,
    )
    for copy in copies[:3]:
        copy.wait()
    letters = letters_ref[...]
    rows = gathered_rows(taps_ref[...].astype(F32).reshape(16, 1024).astype(BF16))
    stacked = []
    for m in range(8):
        block = rows[m // 2][:, 128 * (m % 2) : 128 * (m % 2) + 128].astype(F32)
        stacked.append(jnp.concatenate([block[0:8], block[8:16]], axis=1))
    row, lane = iota((256, 512), 0), iota((1, 512), 1)
    spot = lane & 127
    source = jnp.where(spot < 64, (spot >> 5) * 128 + (lane >> 7) * 32 + (spot & 31), -1)
    spread = jnp.where(row == source, 1.0, 0.0).astype(BF16)
    moved = matmul(jnp.concatenate(stacked, axis=0).astype(BF16), spread)
    line = jnp.broadcast_to(letters.astype(F32), (8, 128))
    which, lane = iota((8, 128), 0), iota((8, 128), 1)
    shown = jnp.where(which == 0, pltpu.roll(line, 64, 1), jnp.where(which == 1, line, 0.0))
    shown = jnp.where(lane >= 64, shown, 0.0)
    for m in range(8):
        for d in range(4):
            piece = moved[8 * m : 8 * m + 8, 128 * d : 128 * d + 128] + shown
            send_ref[4 * m + d, 64:72, :] = piece.astype(BF16)
    square = iota((128, 128), 0) == iota((128, 128), 1)
    letter = jnp.sum(jnp.where(square, letters.astype(F32), 0.0), axis=1, keepdims=True)
    added = embedding_ref[0:1, :]
    for index in range(1, 4):
        added = jnp.where(letter == float(index), embedding_ref[index : index + 1, :], added)
    copies[3].wait()
    send_stretch((hidden_ref[0].astype(F32) + added).astype(BF16), send_ref, 0)
    copies[4].wait()
    copies[5].wait()
    send_stretch((upstream_ref[0].astype(F32) * gate_ref[0].astype(F32)).astype(BF16), send_ref, 32)


def load_pair(ref, base, start, size):
    return tuple(
        [ref[row : row + STEP, lane : lane + LANES] for lane in range(start, start + size, LANES)]
        for row in (base, base + CHUNK)
    )


def with_neighbours(pair, width):
    lane = iota((STEP, LANES), 1)
    sign = (1 - 2 * (iota((STEP, LANES), 0) & 1)).astype(F32)
    if width == LANES // 2:
        high_sign = jnp.where(lane >= width, sign, 0.0)
        low_sign = sign - high_sign
        back, on = [], []
        for first, second in pair:
            turned, other = pltpu.roll(first, width, 1), pltpu.roll(second, width, 1)
            between = sign * jnp.where(lane < width, turned, other)
            back.append([first + high_sign * turned, second + between])
            on.append([first + between, second + low_sign * other])
        return tuple(back), tuple(on)
    lane = iota((STEP, COLS), 1)
    sign = (1 - 2 * (iota((STEP, COLS), 0) & 1)).astype(F32)
    both = []
    for shift, keep in ((width, lane >= width), (COLS - width, lane < COLS - width)):
        signs = jnp.where(keep, sign, 0.0)
        moved = []
        for parts in pair:
            wide = jnp.concatenate(parts, axis=1)
            wide = wide + signs * pltpu.roll(wide, shift, 1)
            moved.append([wide[:, :LANES], wide[:, LANES:]])
        both.append(tuple(moved))
    return tuple(both)


def products(first):
    real_row = iota((STEP, LANES), 0) == 0

    def settle(a, b, real, imaginary):
        if first:
            real = jnp.where(real_row, a[0] * b[0], real)
            imaginary = jnp.where(real_row, a[1] * b[1], imaginary)
        return real, imaginary

    def times(a, b):
        return settle(a, b, a[0] * b[0] - a[1] * b[1], a[0] * b[1] + a[1] * b[0])

    def times_conjugate(a, b):
        return settle(a, b, a[0] * b[0] + a[1] * b[1], a[1] * b[0] - a[0] * b[1])

    return times, times_conjugate


def plus(a, b):
    return a[0] + b[0], a[1] + b[1]


def column(pair, index):
    return pair[0][index], pair[1][index]


def store_split(high_ref, low_ref, base, start, pair):
    for row, part in ((base, 0), (base + CHUNK, 1)):
        high = pair[part].astype(BF16)
        high_ref[row : row + STEP, start : start + LANES] = high
        low_ref[row : row + STEP, start : start + LANES] = (pair[part] - high.astype(F32)).astype(BF16)


def spectra_step(spectra_ref, high_ref, low_ref, narrow, width, base, first):
    times, times_conjugate = products(first)
    back, on = with_neighbours(load_pair(spectra_ref, base, 0, COLS), width)
    own = column(load_pair(spectra_ref, base, 2 * COLS, LANES), 0)
    mirror = column(load_pair(spectra_ref, base, 2 * COLS + LANES, LANES), 0)
    for index in range(2):
        field = plus(times(column(back, index), own), times_conjugate(column(on, index), mirror))
        store_split(high_ref, low_ref, base, LANES * index, field)
    grads = load_pair(spectra_ref, base, COLS, COLS)
    causal, ahead = None, None
    for index in range(2):
        one = times_conjugate(column(grads, index), column(back, index))
        two = times_conjugate(column(on, index), column(grads, index))
        causal = one if causal is None else plus(causal, one)
        ahead = two if ahead is None else plus(ahead, two)
    lags = plus(causal, tuple(pltpu.roll(part, narrow // 2, 1) for part in ahead))
    store_split(high_ref, low_ref, base, 2 * COLS, lags)
    back, on = with_neighbours(grads, width)
    for index in range(2):
        wanted = plus(times(column(back, index), mirror), times_conjugate(column(on, index), own))
        store_split(high_ref, low_ref, base, COLS + LANES * index, wanted)


def transforms(samples_ref, table_refs, copies, spectra_ref, high_ref, low_ref, result_ref, narrow, width):
    forward_high, forward_low, backward_high, backward_low = table_refs
    chunks = BLOCK // CHUNK

    def forward(chunk):
        rows = slice(2 * CHUNK * chunk, 2 * CHUNK * (chunk + 1))
        for columns in (slice(0, COLS), slice(2 * COLS, 3 * COLS), slice(COLS, 2 * COLS)):
            spectra_ref[rows, columns] = matmul(forward_high[rows, :], samples_ref[:, columns]) + matmul(
                forward_low[rows, :], samples_ref[:, columns]
            )

    forward(0)
    for chunk in range(chunks):
        if chunk + 1 < chunks:
            forward(chunk + 1)
        for base in range(2 * CHUNK * chunk, 2 * CHUNK * chunk + CHUNK, STEP):
            spectra_step(spectra_ref, high_ref, low_ref, narrow, width, base, base == 0)
        if chunk + 1 == GROUP:
            for copy in copies:
                copy.wait()
        if (chunk + 1) % GROUP == 0:
            span = slice(2 * CHUNK * (chunk + 1 - GROUP), 2 * CHUNK * (chunk + 1))
            for columns in (slice(0, COLS), slice(COLS, 2 * COLS), slice(2 * COLS, 2 * COLS + LANES)):
                made = (
                    matmul(backward_high[:, span], high_ref[span, columns])
                    + matmul(backward_low[:, span], high_ref[span, columns])
                    + matmul(backward_high[:, span], low_ref[span, columns])
                )
                result_ref[:, columns] = made if chunk + 1 == GROUP else result_ref[:, columns] + made


def column_sum(total, narrow):
    shift = LANES // 2
    while shift >= narrow:
        total = total + pltpu.roll(total, shift, 1)
        shift //= 2
    return total


def letter_sums(values_grad, choice, belongs, narrow):
    high = values_grad.astype(BF16)
    low = (values_grad - high.astype(F32)).astype(BF16)
    sums = jnp.where(belongs, matmul(choice, high) + matmul(choice, low), 0.0)
    groups = sums.shape[0] // 4
    rows = [jnp.sum(sums[groups * a : groups * a + groups], axis=0, keepdims=True) for a in range(4)]
    total = jnp.concatenate(rows, axis=0)
    return column_sum(total[:, :LANES] + total[:, LANES:], narrow)


PLACES = [(u, s) for u in range(2) for s in range(4)]


def unpack_block(receive_ref, place, samples_ref, lanes):
    stacked = []
    for u, s in PLACES:
        pieces = [
            receive_ref[16 * d + 4 * (2 * u + j) + s, place : place + 32, :] for j in range(2) for d in range(2)
        ]
        stacked.append(jnp.concatenate(pieces, axis=1))
    moved = matmul(jnp.concatenate(stacked, axis=0), swap_matrix()).astype(BF16)
    for index, (u, s) in enumerate(PLACES):
        for q in range(4):
            start = 128 * s + 32 * q
            samples_ref[start : start + 32, lanes + 128 * u : lanes + 128 * u + 128] = moved[
                32 * index : 32 * index + 32, 128 * q : 128 * q + 128
            ]


def pack_block(result_ref, lanes, send_ref, place):
    stacked = []
    for u, s in PLACES:
        pieces = [
            result_ref[128 * s + 32 * q : 128 * s + 32 * q + 32, lanes + 128 * u : lanes + 128 * u + 128]
            for q in range(4)
        ]
        stacked.append(jnp.concatenate(pieces, axis=1).astype(BF16))
    moved = matmul(jnp.concatenate(stacked, axis=0), swap_matrix()).astype(BF16)
    for index, (u, s) in enumerate(PLACES):
        for j in range(2):
            for d in range(2):
                group = 2 * j + d
                send_ref[16 * d + 4 * (2 * u + j) + s, place : place + 32, :] = moved[
                    32 * index : 32 * index + 32, 128 * group : 128 * group + 128
                ]


def unpack_taps(tails, samples_ref):
    row, lane = iota((128, 256), 0), iota((1, 256), 1)
    spot = (lane & 31) ^ ((lane >> 7) << 4)
    for d in range(2):
        tail = tails[16 * d : 16 * d + 16].reshape(128, 128).astype(BF16)
        for k in range(2):
            spread = jnp.where(row == 32 * k + spot, 1.0, 0.0).astype(BF16)
            start = 128 * (2 * d + k)
            samples_ref[start : start + 128, 512:768] = matmul(tail, spread).astype(BF16)


def pack_tails(norming, tails, result_ref, send_ref):
    quarter = iota((128, 128), 1) >> 5
    sums = column_sum(result_ref[:, 512:640], 32)
    lags = sums[0:128]
    for k in range(1, 4):
        lags = jnp.where(quarter == k, sums[128 * k : 128 * k + 128], lags)
    lags = (lags * norming).reshape(16, 8, 128).astype(BF16)
    send_ref[0:16, 64:72, :] = lags
    send_ref[16:32, 64:72, :] = lags
    line, source = iota((32, 128), 1), iota((32, 128), 0)
    letters = jnp.where(line < 64, pltpu.roll(tails[:, 0, :], 64, 1), tails[:, 1, :])
    choice = []
    for a in range(4):
        chosen = jnp.where(letters == float(a), 1.0, 0.0)
        choice.append(jnp.concatenate([jnp.where((source & 3) == s, chosen, 0.0) for s in range(4)], axis=1))
    choice = jnp.concatenate(choice, axis=0).astype(BF16)
    source = iota((128, 256), 0) & 31
    belongs = (((source >> 2) & 3) * 2 + (source >> 4)) == (iota((128, 256), 1) >> 5)
    sums = letter_sums(result_ref[:, 256:512], choice, belongs, 32) * norming
    high = sums.astype(BF16).astype(F32)
    tile = jnp.concatenate([high, sums - high], axis=0).astype(BF16)
    for index in range(32):
        send_ref[index, 72:80, :] = tile


def middle_kernel(
    norming, receive_ref, fh_ref, fl_ref, bh_hbm, bl_hbm, send_ref,
    bh_ref, bl_ref, sems, samples_ref, spectra_ref, high_ref, low_ref, result_ref,
):
    table_refs = (fh_ref, fl_ref, bh_ref, bl_ref)
    copies = copy_in([(bh_hbm, bh_ref), (bl_hbm, bl_ref)], sems)
    unpack_block(receive_ref, 0, samples_ref, 0)
    tails = receive_ref[:, 64:72, :].astype(F32)
    unpack_taps(tails, samples_ref)
    unpack_block(receive_ref, 32, samples_ref, 256)
    transforms(samples_ref, table_refs, copies, spectra_ref, high_ref, low_ref, result_ref, 32, 64)
    pack_block(result_ref, 0, send_ref, 0)
    pack_block(result_ref, 256, send_ref, 32)
    pack_tails(norming, tails, result_ref, send_ref)


def received_columns(receive_ref, place):
    stacked = []
    for m in range(8):
        pieces = [receive_ref[4 * m + d, place : place + 32, :] for d in range(4)]
        stacked.append(jnp.concatenate(pieces, axis=1))
    moved = matmul(jnp.concatenate(stacked, axis=0), swap_matrix()).astype(BF16)
    back = return_channels()
    result = []
    for u in range(4):
        columns = []
        for m in (2 * u, 2 * u + 1):
            rows = [moved[32 * m : 32 * m + 32, 128 * q : 128 * q + 128] for q in range(4)]
            columns.append(jnp.concatenate(rows, axis=0))
        result.append(matmul(jnp.concatenate(columns, axis=1), back))
    return result


def places_of(u):
    return ((slice(128 * u, 128 * u + 128), slice(0, 128)), (slice(896 - 128 * u, 1024 - 128 * u), slice(128, 256)))


def finish_kernel(receive_ref, gate_ref, upstream_ref, out_ref, hidden_ref, gated_ref, filter_ref, embedding_ref):
    for u, field in enumerate(received_columns(receive_ref, 0)):
        for there, here in places_of(u):
            out_ref[0, :, there] = (gate_ref[0, :, there].astype(F32) * field[:, here]).astype(BF16)
            gated_ref[0, :, there] = (upstream_ref[0, :, there].astype(F32) * field[:, here]).astype(BF16)
    for u, rows in enumerate(received_columns(receive_ref, 32)):
        for there, here in places_of(u):
            hidden_ref[0, :, there] = rows[:, here].astype(BF16)
    back = return_channels()
    tails = receive_ref[:, 64:80, :].astype(F32)
    stacked = [jnp.concatenate([tails[4 * m + d, 0:8, :] for d in range(4)], axis=1) for m in range(8)]
    moved = matmul(jnp.concatenate(stacked, axis=0).astype(BF16), swap_matrix())
    quarter = iota((8, 128), 1) >> 5
    for u in range(4):
        columns = []
        for m in (2 * u, 2 * u + 1):
            rows = [moved[8 * m : 8 * m + 8, 128 * k : 128 * k + 128] for k in range(4)]
            sums = tails[4 * m, 8:16, :]
            for d in range(1, 4):
                sums = jnp.where(quarter == d, tails[4 * m + d, 8:16, :], sums)
            columns.append(jnp.concatenate(rows + [sums], axis=0))
        done = matmul(jnp.concatenate(columns, axis=1).astype(BF16), back)
        for there, here in places_of(u):
            filter_ref[:, :, there] = done[0:32, here].reshape(4, 8, 128)
            embedding_ref[:, there] = done[32:36, here] + done[36:40, here]


WORK = [
    pltpu.VMEM((BLOCK, 2 * BLOCK), BF16),
    pltpu.VMEM((BLOCK, 2 * BLOCK), BF16),
    pltpu.SemaphoreType.DMA((2,)),
    pltpu.VMEM((BLOCK, 3 * COLS), BF16),
    pltpu.VMEM((2 * BLOCK, 3 * COLS), F32),
    pltpu.VMEM((2 * BLOCK, 2 * COLS + LANES), BF16),
    pltpu.VMEM((2 * BLOCK, 2 * COLS + LANES), BF16),
    pltpu.VMEM((BLOCK, 2 * COLS + LANES), F32),
]
VM = pl.BlockSpec(memory_space=pltpu.VMEM)
HBM = pl.BlockSpec(memory_space=pltpu.HBM)


def shape_of(*dims, dtype=BF16):
    return jax.ShapeDtypeStruct(dims, dtype)


def call(kernel, specs, shapes, scratch=(), mebibytes=32):
    return pl.pallas_call(
        kernel,
        in_specs=specs,
        out_shape=shapes,
        scratch_shapes=scratch,
        compiler_params=pltpu.CompilerParams(vmem_limit_bytes=mebibytes * 1024 * 1024),
    )


def in_hbm(array):
    return pltpu.with_memory_space_constraint(array, pltpu.HBM)


def placed_tables():
    fh, fl, bh, bl = tables()
    return fh, fl, in_hbm(bh), in_hbm(bl)


def exchange(array):
    return lax.all_to_all(array, ("dp", "seq"), 0, 0, tiled=True)


def packed_device(hidden, letters, gate_input, cotangent, embedding, filter_taps, norming):
    stretch = pltpu.VMEM(hidden.shape, BF16)
    sent = call(
        pack_kernel,
        [HBM] * 6,
        shape_of(32, 72, 128),
        [
            stretch,
            pltpu.VMEM(letters.shape, jnp.int32),
            stretch,
            stretch,
            pltpu.VMEM(embedding.shape, F32),
            pltpu.VMEM((2, 8, 1024), BF16),
            pltpu.SemaphoreType.DMA((6,)),
        ],
        16,
    )(*(in_hbm(array) for array in (hidden, letters, gate_input, cotangent, embedding, filter_taps)))
    here = exchange(sent)
    def kernel(*refs):
        middle_kernel(norming, *refs)

    sent = call(
        kernel,
        [VM] * 3 + [HBM] * 2,
        shape_of(32, 80, 128),
        WORK,
        24,
    )(here, *placed_tables())
    here = exchange(sent)
    shape = jax.ShapeDtypeStruct(hidden.shape, BF16)
    return call(
        finish_kernel,
        [VM] * 3,
        (shape, shape, shape, shape_of(*filter_taps.shape, dtype=F32), shape_of(*embedding.shape, dtype=F32)),
        (),
        16,
    )(here, gate_input, cotangent)


def plain_kernel(
    narrow, width, letters_ref, given_ref, fh_ref, fl_ref, bh_hbm, bl_hbm, field_ref, back_ref, lags_ref, sums_ref,
    bh_ref, bl_ref, sems, samples_ref, spectra_ref, high_ref, low_ref, result_ref,
):
    table_refs = (fh_ref, fl_ref, bh_ref, bl_ref)
    copies = copy_in([(bh_hbm, bh_ref), (bl_hbm, bl_ref)], sems)
    samples_ref[...] = given_ref[...]
    transforms(samples_ref, table_refs, copies, spectra_ref, high_ref, low_ref, result_ref, narrow, width)
    field_ref[...] = result_ref[:, 0:COLS].astype(BF16)
    back_ref[...] = result_ref[:, COLS : 2 * COLS].astype(BF16)
    lags_ref[...] = column_sum(result_ref[:, 2 * COLS :], narrow)
    letters = letters_ref[...]
    groups = COLS // narrow
    choice = jnp.concatenate(
        [jnp.where(letters == float(a), 1.0, 0.0) for a in range(4)], axis=0
    ).astype(BF16)
    shape = (4 * groups, COLS)
    belongs = (iota(shape, 0) & (groups - 1)) == iota(shape, 1) // narrow
    sums_ref[...] = letter_sums(result_ref[:, COLS : 2 * COLS], choice, belongs, narrow)


def plain_device(hidden, letters, gate_input, cotangent, embedding, filter_taps, norming):
    axes = ("dp", "seq")
    copies, stretches = lax.axis_size("dp"), lax.axis_size("seq")
    devices = copies * stretches
    stretch, channels = hidden.shape[1], hidden.shape[2]
    narrow = channels // devices
    half = narrow // 2
    blocks = stretch * stretches // BLOCK
    low = np.arange(channels // 2).reshape(devices, half)
    order = np.concatenate([low, channels - 1 - low], axis=1).reshape(-1)
    restore = np.argsort(order)
    onehot = (letters[0][:, None] == jnp.arange(embedding.shape[0], dtype=jnp.int32)[None, :]).astype(F32)
    added = jnp.dot(onehot, embedding, precision=lax.Precision.HIGHEST)
    values = (hidden[0].astype(F32) + added).astype(BF16)
    gate_wide, upstream = gate_input[0].astype(F32), cotangent[0].astype(F32)
    field_grad = (upstream * gate_wide).astype(BF16)

    def scatter(array):
        parts = jnp.take(array, order, axis=1).reshape(stretch, devices, narrow).swapaxes(0, 1)
        parts = lax.all_to_all(parts, axes, 0, 0, tiled=True)
        parts = parts.reshape(copies, blocks, BLOCK, narrow)
        return parts.transpose(2, 1, 0, 3).reshape(BLOCK, COLS)

    def gather(columns):
        parts = columns.reshape(BLOCK, blocks, copies, narrow).transpose(2, 1, 0, 3)
        parts = parts.reshape(devices, stretch, narrow)
        parts = lax.all_to_all(parts, axes, 0, 0, tiled=True)
        return jnp.take(parts.swapaxes(0, 1).reshape(stretch, channels), restore, axis=1)

    taps = lax.all_gather(filter_taps, "seq", axis=1, tiled=True).reshape(BLOCK, channels)
    mine = lax.axis_index("dp") * stretches + lax.axis_index("seq")
    own = lax.dynamic_slice_in_dim(jnp.take(taps, order, axis=1), mine * narrow, narrow, axis=1)
    mirror = jnp.roll(own, half, axis=1)
    repeats = LANES // narrow
    samples = jnp.concatenate(
        [scatter(values), scatter(field_grad), jnp.tile(own, (1, repeats)), jnp.tile(mirror, (1, repeats))], axis=1
    )
    marks = lax.all_gather(letters[0].astype(F32), axes, tiled=True)
    marks = marks.reshape(copies, blocks, BLOCK).swapaxes(0, 1).reshape(copies * blocks, BLOCK)

    def kernel(*refs):
        plain_kernel(narrow, copies * narrow, *refs)

    field, back, lags, sums = call(
        kernel,
        [VM] * 4 + [HBM] * 2,
        (
            shape_of(BLOCK, COLS),
            shape_of(BLOCK, COLS),
            shape_of(BLOCK, LANES, dtype=F32),
            shape_of(embedding.shape[0], LANES, dtype=F32),
        ),
        WORK,
    )(marks, samples, *placed_tables())
    small = jnp.concatenate([lags[:, :narrow], sums[:, :narrow]], axis=0) * norming
    small = jnp.take(lax.all_gather(small, axes, axis=1, tiled=True), restore, axis=1)
    rows = filter_taps.shape[1]
    filter_grad = lax.dynamic_slice_in_dim(
        small[:BLOCK].reshape(filter_taps.shape[0], stretch, channels), lax.axis_index("seq") * rows, rows, axis=1
    )
    field_rows, grad_rows = gather(field).astype(F32), gather(back)
    output = (gate_wide * field_rows).astype(BF16)[None]
    gate_grad = (upstream * field_rows).astype(BF16)[None]
    return output, grad_rows[None], gate_grad, filter_grad, small[BLOCK:]


def per_device(hidden, letters, gate_input, cotangent, embedding, filter_taps):
    copies, stretches = lax.axis_size("dp"), lax.axis_size("seq")
    norming = 1.0 / math.sqrt(copies * hidden.shape[0] * hidden.shape[1] * stretches)
    device = packed_device if (copies, stretches) == (2, 16) else plain_device
    return device(hidden, letters, gate_input, cotangent, embedding, filter_taps, norming)


def solution(mesh):
    return jax.shard_map(
        per_device,
        mesh=mesh,
        in_specs=(
            P("dp", "seq", None),
            P("dp", "seq"),
            P("dp", "seq", None),
            P("dp", "seq", None),
            P(),
            P(None, "seq", None),
        ),
        out_specs=(
            P("dp", "seq", None),
            P("dp", "seq", None),
            P("dp", "seq", None),
            P(None, "seq", None),
            P(),
        ),
        check_vma=False,
    )
```

```python
import math

import jax
import jax.numpy as jnp
import numpy as np
from jax import lax
from jax.experimental import pallas as pl
from jax.experimental.pallas import tpu as pltpu
from jax.sharding import PartitionSpec as P

BLOCK = 512
COLS = 256
LANES = 128
STEP = 16
CHUNK = 128
HALF_ROOT = 0.5**0.5

F32 = jnp.float32
BF16 = jnp.bfloat16


def tables():
    index = np.arange(CHUNK)[:, None]
    forward, backward = [], []
    for step, first, inputs in ((4, 0, 2), (4, 2, 2), (8, 1, 1), (8, 5, 1)):
        moment = np.arange(CHUNK * inputs)[None, :]
        phases = (step * index + first) * moment % (2 * BLOCK)
        angles = phases * (np.pi / BLOCK)
        cosines, sines = np.cos(angles), np.sin(angles)
        if inputs == 2:
            lower = -sines
            if first == 0:
                lower[0] = 1.0 - 2.0 * (moment[0] % 2)
            table = np.concatenate([cosines, lower], axis=0)
        else:
            upper = np.concatenate([cosines, sines], axis=1)
            table = np.concatenate([upper, np.concatenate([-sines, cosines], axis=1)], axis=0)
        weights = np.full((2 * CHUNK, 1), 1.0 / BLOCK)
        if first == 0:
            weights[0] = weights[CHUNK] = 0.5 / BLOCK
        forward.append(table)
        backward.append((table * weights).T)

    def halves(parts):
        table = np.concatenate(parts, axis=0)
        high = table.astype(jnp.bfloat16)
        return high, (table - high.astype(np.float64)).astype(jnp.bfloat16)

    return (*halves(forward), *halves(backward))


def iota(shape, axis):
    return lax.broadcasted_iota(jnp.int32, shape, axis)


def matmul(left, right):
    return jnp.dot(left, right, preferred_element_type=F32)


def turn(array, quarters):
    if isinstance(quarters, int) and quarters % 4 == 0:
        return array
    return pltpu.roll(array, 32 * (quarters & 3), 1)


def choose(arrays, offset, shift):
    block = ((iota(arrays[0].shape, 1) >> 5) - shift) & 3
    result = arrays[0]
    for index in range(1, 4):
        result = jnp.where(block == (index + offset) % 4, arrays[index], result)
    return result


def spread(rows, shift):
    turned = [turn(array, q + shift) for q, array in enumerate(rows)]
    return [choose(turned, d, shift) for d in range(4)]


def collect(chunks, shift):
    return [turn(choose(chunks, q, shift), -q - shift) for q in range(4)]


def owner_shift():
    return lax.axis_index("seq") & 3


def stretch_shift():
    return 2 * ((lax.axis_index("seq") >> 2) & 1) + lax.axis_index("dp")


def channel_source(lane):
    group, spot = lane >> 5, lane & 31
    return jnp.where(spot < 16, 16 * group + spot, 271 - 16 * group - spot)


def gather_channels():
    row, lane = iota((256, 256), 0), iota((1, 256), 1)
    return jnp.where(row == channel_source(lane), 1.0, 0.0).astype(BF16)


def return_channels():
    row, lane = iota((256, 1), 0), iota((256, 256), 1)
    return jnp.where(channel_source(row) == lane, 1.0, 0.0).astype(BF16)


def copy_in(pairs, sems):
    copies = [pltpu.make_async_copy(source, target, sems.at[index]) for index, (source, target) in enumerate(pairs)]
    for copy in copies:
        copy.start()
    return copies


def gathered_rows(part, gather):
    columns = []
    for u in range(4):
        pair = jnp.concatenate([part[:, 128 * u : 128 * u + 128], part[:, 896 - 128 * u : 1024 - 128 * u]], axis=1)
        both = matmul(pair, gather)
        columns += [both[:, :LANES], both[:, LANES:]]
    return columns


def send_stretch(part, gather, send_ref, place):
    shift = stretch_shift()
    for m, block in enumerate(gathered_rows(part, gather)):
        for d, chunk in enumerate(spread([block[32 * q : 32 * q + 32] for q in range(4)], shift)):
            send_ref[4 * m + d, place : place + 32, :] = chunk.astype(BF16)


def pack_kernel(
    hidden_hbm, letters_hbm, gate_hbm, upstream_hbm, embedding_hbm, taps_hbm, send_ref,
    hidden_ref, letters_ref, gate_ref, upstream_ref, embedding_ref, taps_ref, sems,
):
    copies = copy_in(
        [
            (letters_hbm, letters_ref),
            (embedding_hbm, embedding_ref),
            (hidden_hbm, hidden_ref),
            (gate_hbm, gate_ref),
            (upstream_hbm, upstream_ref),
            (taps_hbm.at[pl.ds(2 * lax.axis_index("dp"), 2)], taps_ref),
        ],
        sems,
    )
    gather = gather_channels()
    for copy in copies:
        copy.wait()
    letters = letters_ref[...].astype(F32)
    square = iota((128, 128), 0) == iota((128, 128), 1)
    letter = jnp.sum(jnp.where(square, letters, 0.0), axis=1, keepdims=True)
    added = embedding_ref[0:1, :]
    for index in range(1, 4):
        added = jnp.where(letter == float(index), embedding_ref[index : index + 1, :], added)
    send_stretch((hidden_ref[0].astype(F32) + added).astype(BF16), gather, send_ref, 0)
    send_stretch((upstream_ref[0].astype(F32) * gate_ref[0].astype(F32)).astype(BF16), gather, send_ref, 32)
    rows = gathered_rows(taps_ref[...].astype(F32).reshape(16, 1024).astype(BF16), gather)
    line = jnp.broadcast_to(letters, (8, 128))
    which, lane = iota((8, 128), 0), iota((8, 128), 1)
    shown = jnp.where(which == 0, pltpu.roll(line, 64, 1), jnp.where(which == 1, line, 0.0))
    for m, block in enumerate(rows):
        for d in range(4):
            first = turn(block[0:8], (4 - d) % 4)
            second = turn(block[8:16], (5 - d) % 4)
            piece = jnp.where(lane >= 64, shown, jnp.where(lane >= 32, second, first))
            send_ref[4 * m + d, 64:72, :] = piece.astype(BF16)


def load_pair(ref, base, start, size):
    return tuple(
        [ref[row : row + STEP, lane : lane + LANES] for lane in range(start, start + size, LANES)]
        for row in (base, base + CHUNK)
    )


def with_neighbours(pair, width, odd):
    lane = iota((STEP, LANES), 1)

    def added(here, there):
        return here - there if odd else here + there

    if width == LANES // 2:
        back, on = [], []
        for first, second in pair:
            turned, other = pltpu.roll(first, width, 1), pltpu.roll(second, width, 1)
            between = jnp.where(lane < width, turned, other)
            back.append([added(first, jnp.where(lane < width, 0.0, turned)), added(second, between)])
            on.append([added(first, between), added(second, jnp.where(lane < width, other, 0.0))])
        return tuple(back), tuple(on)
    lane = iota((STEP, COLS), 1)
    both = []
    for shift, keep in ((width, lane >= width), (COLS - width, lane < COLS - width)):
        moved = []
        for parts in pair:
            wide = jnp.concatenate(parts, axis=1)
            wide = added(wide, jnp.where(keep, pltpu.roll(wide, shift, 1), 0.0))
            moved.append([wide[:, :LANES], wide[:, LANES:]])
        both.append(tuple(moved))
    return tuple(both)


def products(first):
    real_row = iota((STEP, LANES), 0) == 0

    def settle(a, b, real, imaginary):
        if first:
            real = jnp.where(real_row, a[0] * b[0], real)
            imaginary = jnp.where(real_row, a[1] * b[1], imaginary)
        return real, imaginary

    def times(a, b):
        return settle(a, b, a[0] * b[0] - a[1] * b[1], a[0] * b[1] + a[1] * b[0])

    def times_conjugate(a, b):
        return settle(a, b, a[0] * b[0] + a[1] * b[1], a[1] * b[0] - a[0] * b[1])

    return times, times_conjugate


def plus(a, b):
    return a[0] + b[0], a[1] + b[1]


def column(pair, index):
    return pair[0][index], pair[1][index]


def store_split(high_ref, low_ref, base, start, pair):
    for row, part in ((base, 0), (base + CHUNK, 1)):
        high = pair[part].astype(BF16)
        high_ref[row : row + STEP, start : start + LANES] = high
        low_ref[row : row + STEP, start : start + LANES] = (pair[part] - high.astype(F32)).astype(BF16)


def spectra_step(spectra_ref, high_ref, low_ref, narrow, width, base):
    times, times_conjugate = products(base == 0)
    odd = base >= 4 * CHUNK
    back, on = with_neighbours(load_pair(spectra_ref, base, 0, COLS), width, odd)
    own = column(load_pair(spectra_ref, base, 2 * COLS, LANES), 0)
    mirror = column(load_pair(spectra_ref, base, 2 * COLS + LANES, LANES), 0)
    for index in range(2):
        field = plus(times(column(back, index), own), times_conjugate(column(on, index), mirror))
        store_split(high_ref, low_ref, base, LANES * index, field)
    grads = load_pair(spectra_ref, base, COLS, COLS)
    causal, ahead = None, None
    for index in range(2):
        one = times_conjugate(column(grads, index), column(back, index))
        two = times_conjugate(column(on, index), column(grads, index))
        causal = one if causal is None else plus(causal, one)
        ahead = two if ahead is None else plus(ahead, two)
    lags = plus(causal, tuple(pltpu.roll(part, narrow // 2, 1) for part in ahead))
    for row, part in ((base, lags[0]), (base + CHUNK, lags[1])):
        high = part.astype(BF16)
        high_ref[row : row + STEP, 2 * COLS : 2 * COLS + LANES] = high
        high_ref[row : row + STEP, 2 * COLS + LANES : 3 * COLS] = (part - high.astype(F32)).astype(BF16)
    back, on = with_neighbours(grads, width, odd)
    for index in range(2):
        wanted = plus(times(column(back, index), mirror), times_conjugate(column(on, index), own))
        store_split(high_ref, low_ref, base, COLS + LANES * index, wanted)


def fold(quarters):
    one, two, three, four = quarters
    between, both = HALF_ROOT * (two - four), HALF_ROOT * (two + four)
    return [one + three, two + four, one - three, two - four, one + between, -three - both, one - between, both - three]


def unfold(parts):
    between, both = HALF_ROOT * (parts[4] - parts[6]), HALF_ROOT * (parts[5] - parts[7])
    one, two = parts[0] + parts[2], parts[1] + parts[3]
    three, four = parts[0] - parts[2], parts[1] - parts[3]
    return [
        one + (parts[4] + parts[6]),
        two + (between - both),
        three - (parts[5] + parts[7]),
        four - (between + both),
    ]


def store_folded(high_ref, low_ref, row, lane, quarters):
    rows, lanes = quarters[0].shape
    for index, part in enumerate(fold(quarters)):
        start = CHUNK * index + row
        high = part.astype(BF16)
        high_ref[start : start + rows, lane : lane + lanes] = high
        low_ref[start : start + rows, lane : lane + lanes] = (part - high.astype(F32)).astype(BF16)


def transforms(inputs, table_refs, spectra_ref, high_ref, low_ref, classes_ref, result_ref, narrow, width):
    inputs_high, inputs_low = inputs
    forward_high, forward_low, backward_high, backward_low = table_refs
    chunks = BLOCK // CHUNK

    def rows_of(chunk):
        return slice(2 * CHUNK * chunk, 2 * CHUNK * (chunk + 1))

    def forward(chunk):
        rows = rows_of(chunk)
        for start in (0, 2 * COLS, COLS):
            columns = slice(start, start + COLS)
            spectra_ref[rows, columns] = (
                matmul(forward_high[rows, :], inputs_high[rows, columns])
                + matmul(forward_low[rows, :], inputs_high[rows, columns])
                + matmul(forward_high[rows, :], inputs_low[rows, columns])
            )

    def backward(chunk):
        rows = rows_of(chunk)
        for start in (COLS, 2 * COLS, 0):
            columns = slice(start, start + COLS)
            made = matmul(backward_high[rows, :], high_ref[rows, columns]) + matmul(
                backward_low[rows, :], high_ref[rows, columns]
            )
            if start < 2 * COLS:
                classes_ref[rows, columns] = made + matmul(backward_high[rows, :], low_ref[rows, columns])
            else:
                classes_ref[rows, start : start + LANES] = made[:, :LANES] + made[:, LANES:]

    forward(0)
    for chunk in range(chunks):
        if chunk + 1 < chunks:
            forward(chunk + 1)
        for base in range(2 * CHUNK * chunk, 2 * CHUNK * chunk + CHUNK, STEP):
            spectra_step(spectra_ref, high_ref, low_ref, narrow, width, base)
        backward(chunk)
    for lane in (COLS, COLS + LANES, 2 * COLS, 0, LANES):
        lanes = slice(lane, lane + LANES)
        for row in range(0, CHUNK, 32):
            parts = [classes_ref[CHUNK * index + row : CHUNK * index + row + 32, lanes] for index in range(8)]
            for quarter, part in enumerate(unfold(parts)):
                result_ref[CHUNK * quarter + row : CHUNK * quarter + row + 32, lanes] = part


def column_sum(total, narrow):
    shift = LANES // 2
    while shift >= narrow:
        total = total + pltpu.roll(total, shift, 1)
        shift //= 2
    return total


def letter_sums(values_grad, choice, belongs, narrow):
    high = values_grad.astype(BF16)
    low = (values_grad - high.astype(F32)).astype(BF16)
    sums = jnp.where(belongs, matmul(choice, high) + matmul(choice, low), 0.0)
    groups = sums.shape[0] // 4
    rows = [jnp.sum(sums[groups * a : groups * a + groups], axis=0, keepdims=True) for a in range(4)]
    total = jnp.concatenate(rows, axis=0)
    return column_sum(total[:, :LANES] + total[:, LANES:], narrow)


PLACES = [(u, s) for u in range(2) for s in range(4)]


def unpack_block(receive_ref, place, high_ref, low_ref, lanes):
    shift = owner_shift()
    for u in range(2):
        stretches = []
        for s in range(4):
            chunks = [
                receive_ref[16 * d + 4 * (2 * u + j) + s, place : place + 32, :].astype(F32)
                for j in range(2)
                for d in range(2)
            ]
            stretches.append(collect(chunks, shift))
        for q in range(4):
            store_folded(high_ref, low_ref, 32 * q, lanes + 128 * u, [rows[q] for rows in stretches])


def pack_block(result_ref, lanes, send_ref, place):
    shift = owner_shift()
    for u, s in PLACES:
        rows = [
            result_ref[128 * s + 32 * q : 128 * s + 32 * q + 32, lanes + 128 * u : lanes + 128 * u + 128]
            for q in range(4)
        ]
        for group, chunk in enumerate(spread(rows, shift)):
            j, d = group // 2, group % 2
            send_ref[16 * d + 4 * (2 * u + j) + s, place : place + 32, :] = chunk.astype(BF16)


def unpack_taps(tails, high_ref, low_ref):
    row, lane = iota((128, 256), 0), iota((1, 256), 1)
    spot = (lane & 31) ^ ((lane >> 7) << 4)
    quarters = []
    for d in range(2):
        tail = tails[16 * d : 16 * d + 16].reshape(128, 128).astype(BF16)
        for k in range(2):
            quarters.append(matmul(tail, jnp.where(row == 32 * k + spot, 1.0, 0.0).astype(BF16)))
    store_folded(high_ref, low_ref, 0, 512, quarters)


def pack_tails(norming, tails, result_ref, send_ref):
    quarter = ((iota((128, 128), 1) >> 5) - lax.axis_index("seq")) & 3
    sums = column_sum(result_ref[:, 512:640], 32)
    lags = sums[0:128]
    for k in range(1, 4):
        lags = jnp.where(quarter == k, sums[128 * k : 128 * k + 128], lags)
    lags = (lags * norming).reshape(16, 8, 128).astype(BF16)
    send_ref[0:16, 64:72, :] = lags
    send_ref[16:32, 64:72, :] = lags
    line, source = iota((32, 128), 1), iota((32, 128), 0)
    letters = jnp.where(line < 64, pltpu.roll(tails[:, 0, :], 64, 1), tails[:, 1, :])
    choice = []
    for a in range(4):
        chosen = jnp.where(letters == float(a), 1.0, 0.0)
        choice.append(jnp.concatenate([jnp.where((source & 3) == s, chosen, 0.0) for s in range(4)], axis=1))
    choice = jnp.concatenate(choice, axis=0).astype(BF16)
    source = iota((128, 256), 0) & 31
    belongs = (((source >> 2) & 3) * 2 + (source >> 4)) == (iota((128, 256), 1) >> 5)
    sums = letter_sums(result_ref[:, 256:512], choice, belongs, 32) * norming
    high = sums.astype(BF16).astype(F32)
    tile = jnp.concatenate([high, sums - high], axis=0).astype(BF16)
    for index in range(32):
        send_ref[index, 72:80, :] = tile


def middle_kernel(
    norming, receive_ref, fh_ref, fl_ref, bh_ref, bl_ref, send_ref,
    inputs_high_ref, inputs_low_ref, spectra_ref, high_ref, low_ref, classes_ref, result_ref,
):
    tails = receive_ref[:, 64:72, :].astype(F32)
    unpack_taps(tails, inputs_high_ref, inputs_low_ref)
    unpack_block(receive_ref, 0, inputs_high_ref, inputs_low_ref, 0)
    unpack_block(receive_ref, 32, inputs_high_ref, inputs_low_ref, 256)
    transforms(
        (inputs_high_ref, inputs_low_ref), (fh_ref, fl_ref, bh_ref, bl_ref),
        spectra_ref, high_ref, low_ref, classes_ref, result_ref, 32, 64,
    )
    pack_tails(norming, tails, result_ref, send_ref)
    pack_block(result_ref, 256, send_ref, 32)
    pack_block(result_ref, 0, send_ref, 0)


def received_columns(receive_ref, place, back):
    shift = stretch_shift()
    result = []
    for u in range(4):
        columns = []
        for m in (2 * u, 2 * u + 1):
            chunks = [receive_ref[4 * m + d, place : place + 32, :].astype(F32) for d in range(4)]
            columns.append(jnp.concatenate(collect(chunks, shift), axis=0).astype(BF16))
        result.append(matmul(jnp.concatenate(columns, axis=1), back))
    return result


def places_of(u):
    return ((slice(128 * u, 128 * u + 128), slice(0, 128)), (slice(896 - 128 * u, 1024 - 128 * u), slice(128, 256)))


def finish_kernel(receive_ref, gate_ref, upstream_ref, out_ref, hidden_ref, gated_ref, filter_ref, embedding_ref):
    back = return_channels()
    for u, field in enumerate(received_columns(receive_ref, 0, back)):
        for there, here in places_of(u):
            out_ref[0, :, there] = (gate_ref[0, :, there].astype(F32) * field[:, here]).astype(BF16)
            gated_ref[0, :, there] = (upstream_ref[0, :, there].astype(F32) * field[:, here]).astype(BF16)
    for u, rows in enumerate(received_columns(receive_ref, 32, back)):
        for there, here in places_of(u):
            hidden_ref[0, :, there] = rows[:, here].astype(BF16)
    tails = receive_ref[:, 64:80, :].astype(F32)
    for u in range(4):
        columns = []
        for m in (2 * u, 2 * u + 1):
            rows = collect([tails[4 * m + d, 0:8, :] for d in range(4)], 0)
            sums = choose([tails[4 * m + d, 8:16, :] for d in range(4)], 0, 0)
            columns.append(jnp.concatenate(rows + [sums], axis=0))
        done = matmul(jnp.concatenate(columns, axis=1).astype(BF16), back)
        for there, here in places_of(u):
            filter_ref[:, :, there] = done[0:32, here].reshape(4, 8, 128)
            embedding_ref[:, there] = done[32:36, here] + done[36:40, here]


WORK = [
    pltpu.VMEM((2 * BLOCK, 3 * COLS), BF16),
    pltpu.VMEM((2 * BLOCK, 3 * COLS), BF16),
    pltpu.VMEM((2 * BLOCK, 3 * COLS), F32),
    pltpu.VMEM((2 * BLOCK, 3 * COLS), BF16),
    pltpu.VMEM((2 * BLOCK, 2 * COLS), BF16),
    pltpu.VMEM((2 * BLOCK, 2 * COLS + LANES), F32),
    pltpu.VMEM((BLOCK, 2 * COLS + LANES), F32),
]
VM = pl.BlockSpec(memory_space=pltpu.VMEM)
HBM = pl.BlockSpec(memory_space=pltpu.HBM)


def shape_of(*dims, dtype=BF16):
    return jax.ShapeDtypeStruct(dims, dtype)


def call(kernel, specs, shapes, scratch=(), mebibytes=32):
    return pl.pallas_call(
        kernel,
        in_specs=specs,
        out_shape=shapes,
        scratch_shapes=scratch,
        compiler_params=pltpu.CompilerParams(vmem_limit_bytes=mebibytes * 1024 * 1024),
    )


def in_hbm(array):
    return pltpu.with_memory_space_constraint(array, pltpu.HBM)


def exchange(array):
    return lax.all_to_all(array, ("dp", "seq"), 0, 0, tiled=True)


def packed_device(hidden, letters, gate_input, cotangent, embedding, filter_taps, norming):
    stretch = pltpu.VMEM(hidden.shape, BF16)
    sent = call(
        pack_kernel,
        [HBM] * 6,
        shape_of(32, 72, 128),
        [
            stretch,
            pltpu.VMEM(letters.shape, jnp.int32),
            stretch,
            stretch,
            pltpu.VMEM(embedding.shape, F32),
            pltpu.VMEM((2, 8, 1024), BF16),
            pltpu.SemaphoreType.DMA((6,)),
        ],
        16,
    )(*(in_hbm(array) for array in (hidden, letters, gate_input, cotangent, embedding, filter_taps)))
    here = exchange(sent)
    def kernel(*refs):
        middle_kernel(norming, *refs)

    sent = call(
        kernel,
        [VM] * 5,
        shape_of(32, 80, 128),
        WORK,
        24,
    )(here, *tables())
    here = exchange(sent)
    shape = jax.ShapeDtypeStruct(hidden.shape, BF16)
    return call(
        finish_kernel,
        [VM] * 3,
        (shape, shape, shape, shape_of(*filter_taps.shape, dtype=F32), shape_of(*embedding.shape, dtype=F32)),
        (),
        16,
    )(here, gate_input, cotangent)


def plain_kernel(
    narrow, width, letters_ref, samples_ref, fh_ref, fl_ref, bh_ref, bl_ref, field_ref, back_ref, lags_ref, sums_ref,
    inputs_high_ref, inputs_low_ref, spectra_ref, high_ref, low_ref, classes_ref, result_ref,
):
    for lane in range(0, 3 * COLS, LANES):
        quarters = [samples_ref[row : row + CHUNK, lane : lane + LANES].astype(F32) for row in range(0, BLOCK, CHUNK)]
        store_folded(inputs_high_ref, inputs_low_ref, 0, lane, quarters)
    transforms(
        (inputs_high_ref, inputs_low_ref), (fh_ref, fl_ref, bh_ref, bl_ref),
        spectra_ref, high_ref, low_ref, classes_ref, result_ref, narrow, width,
    )
    field_ref[...] = result_ref[:, 0:COLS].astype(BF16)
    back_ref[...] = result_ref[:, COLS : 2 * COLS].astype(BF16)
    lags_ref[...] = column_sum(result_ref[:, 2 * COLS :], narrow)
    letters = letters_ref[...]
    groups = COLS // narrow
    choice = jnp.concatenate(
        [jnp.where(letters == float(a), 1.0, 0.0) for a in range(4)], axis=0
    ).astype(BF16)
    shape = (4 * groups, COLS)
    belongs = (iota(shape, 0) & (groups - 1)) == iota(shape, 1) // narrow
    sums_ref[...] = letter_sums(result_ref[:, COLS : 2 * COLS], choice, belongs, narrow)


def plain_device(hidden, letters, gate_input, cotangent, embedding, filter_taps, norming):
    axes = ("dp", "seq")
    copies, stretches = lax.axis_size("dp"), lax.axis_size("seq")
    devices = copies * stretches
    stretch, channels = hidden.shape[1], hidden.shape[2]
    narrow = channels // devices
    half = narrow // 2
    blocks = stretch * stretches // BLOCK
    low = np.arange(channels // 2).reshape(devices, half)
    order = np.concatenate([low, channels - 1 - low], axis=1).reshape(-1)
    restore = np.argsort(order)
    onehot = (letters[0][:, None] == jnp.arange(embedding.shape[0], dtype=jnp.int32)[None, :]).astype(F32)
    added = jnp.dot(onehot, embedding, precision=lax.Precision.HIGHEST)
    values = (hidden[0].astype(F32) + added).astype(BF16)
    gate_wide, upstream = gate_input[0].astype(F32), cotangent[0].astype(F32)
    field_grad = (upstream * gate_wide).astype(BF16)

    def scatter(array):
        parts = jnp.take(array, order, axis=1).reshape(stretch, devices, narrow).swapaxes(0, 1)
        parts = lax.all_to_all(parts, axes, 0, 0, tiled=True)
        parts = parts.reshape(copies, blocks, BLOCK, narrow)
        return parts.transpose(2, 1, 0, 3).reshape(BLOCK, COLS)

    def gather(columns):
        parts = columns.reshape(BLOCK, blocks, copies, narrow).transpose(2, 1, 0, 3)
        parts = parts.reshape(devices, stretch, narrow)
        parts = lax.all_to_all(parts, axes, 0, 0, tiled=True)
        return jnp.take(parts.swapaxes(0, 1).reshape(stretch, channels), restore, axis=1)

    taps = lax.all_gather(filter_taps, "seq", axis=1, tiled=True).reshape(BLOCK, channels)
    mine = lax.axis_index("dp") * stretches + lax.axis_index("seq")
    own = lax.dynamic_slice_in_dim(jnp.take(taps, order, axis=1), mine * narrow, narrow, axis=1)
    mirror = jnp.roll(own, half, axis=1)
    repeats = LANES // narrow
    samples = jnp.concatenate(
        [scatter(values), scatter(field_grad), jnp.tile(own, (1, repeats)), jnp.tile(mirror, (1, repeats))], axis=1
    )
    marks = lax.all_gather(letters[0].astype(F32), axes, tiled=True)
    marks = marks.reshape(copies, blocks, BLOCK).swapaxes(0, 1).reshape(copies * blocks, BLOCK)

    def kernel(*refs):
        plain_kernel(narrow, copies * narrow, *refs)

    field, back, lags, sums = call(
        kernel,
        [VM] * 6,
        (
            shape_of(BLOCK, COLS),
            shape_of(BLOCK, COLS),
            shape_of(BLOCK, LANES, dtype=F32),
            shape_of(embedding.shape[0], LANES, dtype=F32),
        ),
        WORK,
    )(marks, samples, *tables())
    small = jnp.concatenate([lags[:, :narrow], sums[:, :narrow]], axis=0) * norming
    small = jnp.take(lax.all_gather(small, axes, axis=1, tiled=True), restore, axis=1)
    rows = filter_taps.shape[1]
    filter_grad = lax.dynamic_slice_in_dim(
        small[:BLOCK].reshape(filter_taps.shape[0], stretch, channels), lax.axis_index("seq") * rows, rows, axis=1
    )
    field_rows, grad_rows = gather(field).astype(F32), gather(back)
    output = (gate_wide * field_rows).astype(BF16)[None]
    gate_grad = (upstream * field_rows).astype(BF16)[None]
    return output, grad_rows[None], gate_grad, filter_grad, small[BLOCK:]


def per_device(hidden, letters, gate_input, cotangent, embedding, filter_taps):
    copies, stretches = lax.axis_size("dp"), lax.axis_size("seq")
    norming = 1.0 / math.sqrt(copies * hidden.shape[0] * hidden.shape[1] * stretches)
    device = packed_device if (copies, stretches) == (2, 16) else plain_device
    return device(hidden, letters, gate_input, cotangent, embedding, filter_taps, norming)


def solution(mesh):
    return jax.shard_map(
        per_device,
        mesh=mesh,
        in_specs=(
            P("dp", "seq", None),
            P("dp", "seq"),
            P("dp", "seq", None),
            P("dp", "seq", None),
            P(),
            P(None, "seq", None),
        ),
        out_specs=(
            P("dp", "seq", None),
            P("dp", "seq", None),
            P("dp", "seq", None),
            P(None, "seq", None),
            P(),
        ),
        check_vma=False,
    )
```

```python
import math

import jax
import jax.numpy as jnp
import numpy as np
from jax import lax
from jax.experimental import pallas as pl
from jax.experimental.pallas import tpu as pltpu
from jax.sharding import PartitionSpec as P

BLOCK = 512
COLS = 256
LANES = 128
STEP = 16
CHUNK = 128
HALF_ROOT = 0.5**0.5
CHUNK_ROWS = 74

F32 = jnp.float32
BF16 = jnp.bfloat16


def tables():
    index = np.arange(CHUNK)[:, None]
    forward, backward = [], []
    for step, first, inputs in ((4, 0, 2), (4, 2, 2), (8, 1, 1), (8, 5, 1)):
        moment = np.arange(CHUNK * inputs)[None, :]
        phases = (step * index + first) * moment % (2 * BLOCK)
        angles = phases * (np.pi / BLOCK)
        cosines, sines = np.cos(angles), np.sin(angles)
        if inputs == 2:
            lower = -sines
            if first == 0:
                lower[0] = 1.0 - 2.0 * (moment[0] % 2)
            table = np.concatenate([cosines, lower], axis=0)
        else:
            upper = np.concatenate([cosines, sines], axis=1)
            table = np.concatenate([upper, np.concatenate([-sines, cosines], axis=1)], axis=0)
        weights = np.full((2 * CHUNK, 1), 1.0 / BLOCK)
        if first == 0:
            weights[0] = weights[CHUNK] = 0.5 / BLOCK
        forward.append(table)
        backward.append((table * weights).T)

    def halves(parts):
        table = np.concatenate(parts, axis=0)
        high = table.astype(jnp.bfloat16)
        return high, (table - high.astype(np.float64)).astype(jnp.bfloat16)

    return (*halves(forward), *halves(backward))


def iota(shape, axis):
    return lax.broadcasted_iota(jnp.int32, shape, axis)


def matmul(left, right):
    return jnp.dot(left, right, preferred_element_type=F32)


def turn(array, quarters):
    if isinstance(quarters, int) and quarters % 4 == 0:
        return array
    return pltpu.roll(array, 32 * (quarters & 3), 1)


def choose(arrays, offset, shift):
    block = ((iota(arrays[0].shape, 1) >> 5) - shift) & 3
    result = arrays[0]
    for index in range(1, 4):
        result = jnp.where(block == (index + offset) % 4, arrays[index], result)
    return result


def spread(rows, shift):
    turned = [turn(array, q + shift) for q, array in enumerate(rows)]
    return [choose(turned, d, shift) for d in range(4)]


def collect(chunks, shift):
    return [turn(choose(chunks, q, shift), -q - shift) for q in range(4)]


def owner_shift():
    return lax.axis_index("seq") & 3


def stretch_shift():
    return 2 * ((lax.axis_index("seq") >> 2) & 1) + lax.axis_index("dp")


def channel_source(lane):
    group, spot = lane >> 5, lane & 31
    return jnp.where(spot < 16, 16 * group + spot, 271 - 16 * group - spot)


def gather_channels():
    row, lane = iota((256, 256), 0), iota((1, 256), 1)
    return jnp.where(row == channel_source(lane), 1.0, 0.0).astype(BF16)


def return_channels():
    row, lane = iota((256, 1), 0), iota((256, 256), 1)
    return jnp.where(channel_source(row) == lane, 1.0, 0.0).astype(BF16)


def copy_in(pairs, sems):
    copies = [pltpu.make_async_copy(source, target, sems.at[index]) for index, (source, target) in enumerate(pairs)]
    for copy in copies:
        copy.start()
    return copies


def gathered_rows(part, gather):
    columns = []
    for u in range(4):
        pair = jnp.concatenate([part[:, 128 * u : 128 * u + 128], part[:, 896 - 128 * u : 1024 - 128 * u]], axis=1)
        both = matmul(pair, gather)
        columns += [both[:, :LANES], both[:, LANES:]]
    return columns


def send_stretch(part, gather, send_ref, place):
    shift = stretch_shift()
    for m, block in enumerate(gathered_rows(part, gather)):
        for d, chunk in enumerate(spread([block[32 * q : 32 * q + 32] for q in range(4)], shift)):
            send_ref[4 * m + d, place : place + 32, :] = chunk.astype(BF16)


def pack_kernel(
    hidden_hbm, letters_hbm, gate_hbm, upstream_hbm, embedding_hbm, taps_hbm, send_ref,
    hidden_ref, letters_ref, gate_ref, upstream_ref, embedding_ref, taps_ref, sems,
):
    copies = copy_in(
        [
            (letters_hbm, letters_ref),
            (embedding_hbm, embedding_ref),
            (hidden_hbm, hidden_ref),
            (gate_hbm, gate_ref),
            (upstream_hbm, upstream_ref),
            (taps_hbm.at[pl.ds(2 * lax.axis_index("dp"), 2)], taps_ref),
        ],
        sems,
    )
    gather = gather_channels()
    for copy in copies:
        copy.wait()
    letters = letters_ref[...].astype(F32)
    square = iota((128, 128), 0) == iota((128, 128), 1)
    letter = jnp.sum(jnp.where(square, letters, 0.0), axis=1, keepdims=True)
    added = embedding_ref[0:1, :]
    for index in range(1, 4):
        added = jnp.where(letter == float(index), embedding_ref[index : index + 1, :], added)
    send_stretch((hidden_ref[0].astype(F32) + added).astype(BF16), gather, send_ref, 0)
    send_stretch((upstream_ref[0].astype(F32) * gate_ref[0].astype(F32)).astype(BF16), gather, send_ref, 32)
    rows = gathered_rows(taps_ref[...].astype(F32).reshape(16, 1024).astype(BF16), gather)
    line = jnp.broadcast_to(letters, (8, 128))
    which, lane = iota((8, 128), 0), iota((8, 128), 1)
    shown = jnp.where(which == 0, pltpu.roll(line, 64, 1), jnp.where(which == 1, line, 0.0))
    for m, block in enumerate(rows):
        for d in range(4):
            first = turn(block[0:8], (4 - d) % 4)
            second = turn(block[8:16], (5 - d) % 4)
            piece = jnp.where(lane >= 64, shown, jnp.where(lane >= 32, second, first))
            send_ref[4 * m + d, 64:72, :] = piece.astype(BF16)


def load_pair(ref, base, start, size):
    return tuple(
        [ref[row : row + STEP, lane : lane + LANES] for lane in range(start, start + size, LANES)]
        for row in (base, base + CHUNK)
    )


def with_neighbours(pair, width, odd):
    lane = iota((STEP, LANES), 1)

    def added(here, there):
        return here - there if odd else here + there

    if width == LANES // 2:
        back, on = [], []
        for first, second in pair:
            turned, other = pltpu.roll(first, width, 1), pltpu.roll(second, width, 1)
            between = jnp.where(lane < width, turned, other)
            back.append([added(first, jnp.where(lane < width, 0.0, turned)), added(second, between)])
            on.append([added(first, between), added(second, jnp.where(lane < width, other, 0.0))])
        return tuple(back), tuple(on)
    lane = iota((STEP, COLS), 1)
    both = []
    for shift, keep in ((width, lane >= width), (COLS - width, lane < COLS - width)):
        moved = []
        for parts in pair:
            wide = jnp.concatenate(parts, axis=1)
            wide = added(wide, jnp.where(keep, pltpu.roll(wide, shift, 1), 0.0))
            moved.append([wide[:, :LANES], wide[:, LANES:]])
        both.append(tuple(moved))
    return tuple(both)


def products(first):
    real_row = iota((STEP, LANES), 0) == 0

    def settle(a, b, real, imaginary):
        if first:
            real = jnp.where(real_row, a[0] * b[0], real)
            imaginary = jnp.where(real_row, a[1] * b[1], imaginary)
        return real, imaginary

    def times(a, b):
        return settle(a, b, a[0] * b[0] - a[1] * b[1], a[0] * b[1] + a[1] * b[0])

    def times_conjugate(a, b):
        return settle(a, b, a[0] * b[0] + a[1] * b[1], a[1] * b[0] - a[0] * b[1])

    return times, times_conjugate


def plus(a, b):
    return a[0] + b[0], a[1] + b[1]


def column(pair, index):
    return pair[0][index], pair[1][index]


def store_split(high_ref, low_ref, base, start, pair):
    for row, part in ((base, 0), (base + CHUNK, 1)):
        high = pair[part].astype(BF16)
        high_ref[row : row + STEP, start : start + LANES] = high
        low_ref[row : row + STEP, start : start + LANES] = (pair[part] - high.astype(F32)).astype(BF16)


def spectra_step(spectra_ref, high_ref, low_ref, narrow, width, base):
    times, times_conjugate = products(base == 0)
    odd = base >= 4 * CHUNK
    back, on = with_neighbours(load_pair(spectra_ref, base, 0, COLS), width, odd)
    own = column(load_pair(spectra_ref, base, 2 * COLS, LANES), 0)
    mirror = column(load_pair(spectra_ref, base, 2 * COLS + LANES, LANES), 0)
    for index in range(2):
        field = plus(times(column(back, index), own), times_conjugate(column(on, index), mirror))
        store_split(high_ref, low_ref, base, LANES * index, field)
    grads = load_pair(spectra_ref, base, COLS, COLS)
    causal, ahead = None, None
    for index in range(2):
        one = times_conjugate(column(grads, index), column(back, index))
        two = times_conjugate(column(on, index), column(grads, index))
        causal = one if causal is None else plus(causal, one)
        ahead = two if ahead is None else plus(ahead, two)
    lags = plus(causal, tuple(pltpu.roll(part, narrow // 2, 1) for part in ahead))
    for row, part in ((base, lags[0]), (base + CHUNK, lags[1])):
        high = part.astype(BF16)
        high_ref[row : row + STEP, 2 * COLS : 2 * COLS + LANES] = high
        high_ref[row : row + STEP, 2 * COLS + LANES : 3 * COLS] = (part - high.astype(F32)).astype(BF16)
    back, on = with_neighbours(grads, width, odd)
    for index in range(2):
        wanted = plus(times(column(back, index), mirror), times_conjugate(column(on, index), own))
        store_split(high_ref, low_ref, base, COLS + LANES * index, wanted)


def fold(quarters):
    one, two, three, four = quarters
    between, both = HALF_ROOT * (two - four), HALF_ROOT * (two + four)
    return [one + three, two + four, one - three, two - four, one + between, -three - both, one - between, both - three]


def unfold(parts):
    between, both = HALF_ROOT * (parts[4] - parts[6]), HALF_ROOT * (parts[5] - parts[7])
    one, two = parts[0] + parts[2], parts[1] + parts[3]
    three, four = parts[0] - parts[2], parts[1] - parts[3]
    return [
        one + (parts[4] + parts[6]),
        two + (between - both),
        three - (parts[5] + parts[7]),
        four - (between + both),
    ]


def store_folded(high_ref, low_ref, row, lane, quarters):
    rows, lanes = quarters[0].shape
    for index, part in enumerate(fold(quarters)):
        start = CHUNK * index + row
        high = part.astype(BF16)
        high_ref[start : start + rows, lane : lane + lanes] = high
        low_ref[start : start + rows, lane : lane + lanes] = (part - high.astype(F32)).astype(BF16)


def transforms(inputs, table_refs, spectra_ref, high_ref, low_ref, classes_ref, result_ref, narrow, width):
    inputs_high, inputs_low = inputs
    forward_high, forward_low, backward_high, backward_low = table_refs
    chunks = BLOCK // CHUNK

    def rows_of(chunk):
        return slice(2 * CHUNK * chunk, 2 * CHUNK * (chunk + 1))

    def forward(chunk):
        rows = rows_of(chunk)
        for start in (0, 2 * COLS, COLS):
            columns = slice(start, start + COLS)
            spectra_ref[rows, columns] = (
                matmul(forward_high[rows, :], inputs_high[rows, columns])
                + matmul(forward_low[rows, :], inputs_high[rows, columns])
                + matmul(forward_high[rows, :], inputs_low[rows, columns])
            )

    def backward(chunk):
        rows = rows_of(chunk)
        for start in (COLS, 2 * COLS, 0):
            columns = slice(start, start + COLS)
            made = matmul(backward_high[rows, :], high_ref[rows, columns]) + matmul(
                backward_low[rows, :], high_ref[rows, columns]
            )
            if start < 2 * COLS:
                classes_ref[rows, columns] = made + matmul(backward_high[rows, :], low_ref[rows, columns])
            else:
                classes_ref[rows, start : start + LANES] = made[:, :LANES] + made[:, LANES:]

    forward(0)
    for chunk in range(chunks):
        if chunk + 1 < chunks:
            forward(chunk + 1)
        for base in range(2 * CHUNK * chunk, 2 * CHUNK * chunk + CHUNK, STEP):
            spectra_step(spectra_ref, high_ref, low_ref, narrow, width, base)
        backward(chunk)
    for lane in (COLS, COLS + LANES, 2 * COLS, 0, LANES):
        lanes = slice(lane, lane + LANES)
        for row in range(0, CHUNK, 32):
            parts = [classes_ref[CHUNK * index + row : CHUNK * index + row + 32, lanes] for index in range(8)]
            for quarter, part in enumerate(unfold(parts)):
                result_ref[CHUNK * quarter + row : CHUNK * quarter + row + 32, lanes] = part


def column_sum(total, narrow):
    shift = LANES // 2
    while shift >= narrow:
        total = total + pltpu.roll(total, shift, 1)
        shift //= 2
    return total


def letter_sums(values_grad, choice, belongs, narrow):
    high = values_grad.astype(BF16)
    low = (values_grad - high.astype(F32)).astype(BF16)
    sums = jnp.where(belongs, matmul(choice, high) + matmul(choice, low), 0.0)
    groups = sums.shape[0] // 4
    rows = [jnp.sum(sums[groups * a : groups * a + groups], axis=0, keepdims=True) for a in range(4)]
    total = jnp.concatenate(rows, axis=0)
    return column_sum(total[:, :LANES] + total[:, LANES:], narrow)


PLACES = [(u, s) for u in range(2) for s in range(4)]


def unpack_block(receive_ref, place, high_ref, low_ref, lanes):
    shift = owner_shift()
    for u in range(2):
        stretches = []
        for s in range(4):
            chunks = [
                receive_ref[16 * d + 4 * (2 * u + j) + s, place : place + 32, :].astype(F32)
                for j in range(2)
                for d in range(2)
            ]
            stretches.append(collect(chunks, shift))
        for q in range(4):
            store_folded(high_ref, low_ref, 32 * q, lanes + 128 * u, [rows[q] for rows in stretches])


def put(send_ref, index, pair, rows):
    start = CHUNK_ROWS * index + 2 * pair
    send_ref[start : start + rows.shape[0], :] = rows.astype(BF16)


def take(receive_ref, index, pair, count):
    return receive_ref[index, pair : pair + count].reshape(2 * count, LANES).astype(F32)


def pack_block(result_ref, lanes, send_ref, pair):
    shift = owner_shift()
    for u, s in PLACES:
        rows = [
            result_ref[128 * s + 32 * q : 128 * s + 32 * q + 32, lanes + 128 * u : lanes + 128 * u + 128]
            for q in range(4)
        ]
        for group, chunk in enumerate(spread(rows, shift)):
            j, d = group // 2, group % 2
            put(send_ref, 16 * d + 4 * (2 * u + j) + s, pair, chunk)


def unpack_taps(tails, high_ref, low_ref):
    row, lane = iota((128, 256), 0), iota((1, 256), 1)
    spot = (lane & 31) ^ ((lane >> 7) << 4)
    quarters = []
    for d in range(2):
        tail = tails[16 * d : 16 * d + 16].reshape(128, 128).astype(BF16)
        for k in range(2):
            quarters.append(matmul(tail, jnp.where(row == 32 * k + spot, 1.0, 0.0).astype(BF16)))
    store_folded(high_ref, low_ref, 0, 512, quarters)


def pack_tails(norming, tails, result_ref, send_ref):
    quarter = ((iota((128, 128), 1) >> 5) - lax.axis_index("seq")) & 3
    sums = column_sum(result_ref[:, 512:640], 32)
    lags = sums[0:128]
    for k in range(1, 4):
        lags = jnp.where(quarter == k, sums[128 * k : 128 * k + 128], lags)
    lags = lags * norming
    for index in range(16):
        put(send_ref, index, 32, lags[8 * index : 8 * index + 8])
        put(send_ref, 16 + index, 32, lags[8 * index : 8 * index + 8])
    line, source = iota((32, 128), 1), iota((32, 128), 0)
    letters = jnp.where(line < 64, pltpu.roll(tails[:, 0, :], 64, 1), tails[:, 1, :])
    choice = []
    for a in range(4):
        chosen = jnp.where(letters == float(a), 1.0, 0.0)
        choice.append(jnp.concatenate([jnp.where((source & 3) == s, chosen, 0.0) for s in range(4)], axis=1))
    choice = jnp.concatenate(choice, axis=0).astype(BF16)
    source = iota((128, 256), 0) & 31
    belongs = (((source >> 2) & 3) * 2 + (source >> 4)) == (iota((128, 256), 1) >> 5)
    sums = letter_sums(result_ref[:, 256:512], choice, belongs, 32) * norming
    sums = choose([sums[a : a + 1] for a in range(4)], 0, owner_shift())
    high = sums.astype(BF16).astype(F32)
    tile = jnp.concatenate([high, sums - high], axis=0)
    for index in range(32):
        put(send_ref, index, 36, tile)


def middle_kernel(
    norming, receive_ref, fh_ref, fl_ref, bh_ref, bl_ref, send_ref,
    inputs_high_ref, inputs_low_ref, spectra_ref, high_ref, low_ref, classes_ref, result_ref,
):
    tails = receive_ref[:, 64:72, :].astype(F32)
    unpack_taps(tails, inputs_high_ref, inputs_low_ref)
    unpack_block(receive_ref, 0, inputs_high_ref, inputs_low_ref, 0)
    unpack_block(receive_ref, 32, inputs_high_ref, inputs_low_ref, 256)
    transforms(
        (inputs_high_ref, inputs_low_ref), (fh_ref, fl_ref, bh_ref, bl_ref),
        spectra_ref, high_ref, low_ref, classes_ref, result_ref, 32, 64,
    )
    pack_tails(norming, tails, result_ref, send_ref)
    pack_block(result_ref, 256, send_ref, 16)
    pack_block(result_ref, 0, send_ref, 0)


def received_columns(receive_ref, pair, back):
    shift = stretch_shift()
    result = []
    for u in range(4):
        columns = []
        for m in (2 * u, 2 * u + 1):
            chunks = [take(receive_ref, 4 * m + d, pair, 16) for d in range(4)]
            columns.append(jnp.concatenate(collect(chunks, shift), axis=0).astype(BF16))
        result.append(matmul(jnp.concatenate(columns, axis=1), back))
    return result


def places_of(u):
    return ((slice(128 * u, 128 * u + 128), slice(0, 128)), (slice(896 - 128 * u, 1024 - 128 * u), slice(128, 256)))


def finish_kernel(receive_ref, gate_ref, upstream_ref, out_ref, hidden_ref, gated_ref, filter_ref, embedding_ref):
    back = return_channels()
    for u, field in enumerate(received_columns(receive_ref, 0, back)):
        for there, here in places_of(u):
            out_ref[0, :, there] = (gate_ref[0, :, there].astype(F32) * field[:, here]).astype(BF16)
            gated_ref[0, :, there] = (upstream_ref[0, :, there].astype(F32) * field[:, here]).astype(BF16)
    for u, rows in enumerate(received_columns(receive_ref, 16, back)):
        for there, here in places_of(u):
            hidden_ref[0, :, there] = rows[:, here].astype(BF16)
    for u in range(4):
        columns = []
        for m in (2 * u, 2 * u + 1):
            columns.append(jnp.concatenate(collect([take(receive_ref, 4 * m + d, 32, 4) for d in range(4)], 0), axis=0))
        done = matmul(jnp.concatenate(columns, axis=1).astype(BF16), back)
        for there, here in places_of(u):
            filter_ref[:, :, there] = done[:, here].reshape(4, 8, 128)
    sums = collect(
        [jnp.concatenate([take(receive_ref, 4 * m + d, 36, 1) for m in range(8)], axis=0) for d in range(4)], 0
    )
    rows = []
    for term in range(2):
        for u in range(4):
            for total in sums:
                first, second = total[4 * u + term : 4 * u + term + 1], total[4 * u + 2 + term : 4 * u + 3 + term]
                rows.append(jnp.concatenate([first, second], axis=1))
    done = matmul(jnp.concatenate(rows, axis=0).astype(BF16), back)
    done = done[0:16] + done[16:32]
    for u in range(4):
        for there, here in places_of(u):
            embedding_ref[:, there] = done[4 * u : 4 * u + 4, here]


WORK = [
    pltpu.VMEM((2 * BLOCK, 3 * COLS), BF16),
    pltpu.VMEM((2 * BLOCK, 3 * COLS), BF16),
    pltpu.VMEM((2 * BLOCK, 3 * COLS), F32),
    pltpu.VMEM((2 * BLOCK, 3 * COLS), BF16),
    pltpu.VMEM((2 * BLOCK, 2 * COLS), BF16),
    pltpu.VMEM((2 * BLOCK, 2 * COLS + LANES), F32),
    pltpu.VMEM((BLOCK, 2 * COLS + LANES), F32),
]
VM = pl.BlockSpec(memory_space=pltpu.VMEM)
HBM = pl.BlockSpec(memory_space=pltpu.HBM)


def shape_of(*dims, dtype=BF16):
    return jax.ShapeDtypeStruct(dims, dtype)


def call(kernel, specs, shapes, scratch=(), mebibytes=32):
    return pl.pallas_call(
        kernel,
        in_specs=specs,
        out_shape=shapes,
        scratch_shapes=scratch,
        compiler_params=pltpu.CompilerParams(vmem_limit_bytes=mebibytes * 1024 * 1024),
    )


def in_hbm(array):
    return pltpu.with_memory_space_constraint(array, pltpu.HBM)


def exchange(array):
    return lax.all_to_all(array, ("dp", "seq"), 0, 0, tiled=True)


def packed_device(hidden, letters, gate_input, cotangent, embedding, filter_taps, norming):
    stretch = pltpu.VMEM(hidden.shape, BF16)
    sent = call(
        pack_kernel,
        [HBM] * 6,
        shape_of(32, 72, 128),
        [
            stretch,
            pltpu.VMEM(letters.shape, jnp.int32),
            stretch,
            stretch,
            pltpu.VMEM(embedding.shape, F32),
            pltpu.VMEM((2, 8, 1024), BF16),
            pltpu.SemaphoreType.DMA((6,)),
        ],
        16,
    )(*(in_hbm(array) for array in (hidden, letters, gate_input, cotangent, embedding, filter_taps)))
    here = exchange(sent)
    def kernel(*refs):
        middle_kernel(norming, *refs)

    sent = call(
        kernel,
        [VM] * 5,
        shape_of(32 * CHUNK_ROWS, LANES),
        WORK,
        24,
    )(here, *tables())
    here = exchange(sent.reshape(32, CHUNK_ROWS // 2, 2, LANES))
    shape = jax.ShapeDtypeStruct(hidden.shape, BF16)
    return call(
        finish_kernel,
        [VM] * 3,
        (shape, shape, shape, shape_of(*filter_taps.shape, dtype=F32), shape_of(*embedding.shape, dtype=F32)),
        (),
        16,
    )(here, gate_input, cotangent)


def plain_kernel(
    narrow, width, letters_ref, samples_ref, fh_ref, fl_ref, bh_ref, bl_ref, field_ref, back_ref, lags_ref, sums_ref,
    inputs_high_ref, inputs_low_ref, spectra_ref, high_ref, low_ref, classes_ref, result_ref,
):
    for lane in range(0, 3 * COLS, LANES):
        quarters = [samples_ref[row : row + CHUNK, lane : lane + LANES].astype(F32) for row in range(0, BLOCK, CHUNK)]
        store_folded(inputs_high_ref, inputs_low_ref, 0, lane, quarters)
    transforms(
        (inputs_high_ref, inputs_low_ref), (fh_ref, fl_ref, bh_ref, bl_ref),
        spectra_ref, high_ref, low_ref, classes_ref, result_ref, narrow, width,
    )
    field_ref[...] = result_ref[:, 0:COLS].astype(BF16)
    back_ref[...] = result_ref[:, COLS : 2 * COLS].astype(BF16)
    lags_ref[...] = column_sum(result_ref[:, 2 * COLS :], narrow)
    letters = letters_ref[...]
    groups = COLS // narrow
    choice = jnp.concatenate(
        [jnp.where(letters == float(a), 1.0, 0.0) for a in range(4)], axis=0
    ).astype(BF16)
    shape = (4 * groups, COLS)
    belongs = (iota(shape, 0) & (groups - 1)) == iota(shape, 1) // narrow
    sums_ref[...] = letter_sums(result_ref[:, COLS : 2 * COLS], choice, belongs, narrow)


def plain_device(hidden, letters, gate_input, cotangent, embedding, filter_taps, norming):
    axes = ("dp", "seq")
    copies, stretches = lax.axis_size("dp"), lax.axis_size("seq")
    devices = copies * stretches
    stretch, channels = hidden.shape[1], hidden.shape[2]
    narrow = channels // devices
    half = narrow // 2
    blocks = stretch * stretches // BLOCK
    low = np.arange(channels // 2).reshape(devices, half)
    order = np.concatenate([low, channels - 1 - low], axis=1).reshape(-1)
    restore = np.argsort(order)
    onehot = (letters[0][:, None] == jnp.arange(embedding.shape[0], dtype=jnp.int32)[None, :]).astype(F32)
    added = jnp.dot(onehot, embedding, precision=lax.Precision.HIGHEST)
    values = (hidden[0].astype(F32) + added).astype(BF16)
    gate_wide, upstream = gate_input[0].astype(F32), cotangent[0].astype(F32)
    field_grad = (upstream * gate_wide).astype(BF16)

    def scatter(array):
        parts = jnp.take(array, order, axis=1).reshape(stretch, devices, narrow).swapaxes(0, 1)
        parts = lax.all_to_all(parts, axes, 0, 0, tiled=True)
        parts = parts.reshape(copies, blocks, BLOCK, narrow)
        return parts.transpose(2, 1, 0, 3).reshape(BLOCK, COLS)

    def gather(columns):
        parts = columns.reshape(BLOCK, blocks, copies, narrow).transpose(2, 1, 0, 3)
        parts = parts.reshape(devices, stretch, narrow)
        parts = lax.all_to_all(parts, axes, 0, 0, tiled=True)
        return jnp.take(parts.swapaxes(0, 1).reshape(stretch, channels), restore, axis=1)

    taps = lax.all_gather(filter_taps, "seq", axis=1, tiled=True).reshape(BLOCK, channels)
    mine = lax.axis_index("dp") * stretches + lax.axis_index("seq")
    own = lax.dynamic_slice_in_dim(jnp.take(taps, order, axis=1), mine * narrow, narrow, axis=1)
    mirror = jnp.roll(own, half, axis=1)
    repeats = LANES // narrow
    samples = jnp.concatenate(
        [scatter(values), scatter(field_grad), jnp.tile(own, (1, repeats)), jnp.tile(mirror, (1, repeats))], axis=1
    )
    marks = lax.all_gather(letters[0].astype(F32), axes, tiled=True)
    marks = marks.reshape(copies, blocks, BLOCK).swapaxes(0, 1).reshape(copies * blocks, BLOCK)

    def kernel(*refs):
        plain_kernel(narrow, copies * narrow, *refs)

    field, back, lags, sums = call(
        kernel,
        [VM] * 6,
        (
            shape_of(BLOCK, COLS),
            shape_of(BLOCK, COLS),
            shape_of(BLOCK, LANES, dtype=F32),
            shape_of(embedding.shape[0], LANES, dtype=F32),
        ),
        WORK,
    )(marks, samples, *tables())
    small = jnp.concatenate([lags[:, :narrow], sums[:, :narrow]], axis=0) * norming
    small = jnp.take(lax.all_gather(small, axes, axis=1, tiled=True), restore, axis=1)
    rows = filter_taps.shape[1]
    filter_grad = lax.dynamic_slice_in_dim(
        small[:BLOCK].reshape(filter_taps.shape[0], stretch, channels), lax.axis_index("seq") * rows, rows, axis=1
    )
    field_rows, grad_rows = gather(field).astype(F32), gather(back)
    output = (gate_wide * field_rows).astype(BF16)[None]
    gate_grad = (upstream * field_rows).astype(BF16)[None]
    return output, grad_rows[None], gate_grad, filter_grad, small[BLOCK:]


def per_device(hidden, letters, gate_input, cotangent, embedding, filter_taps):
    copies, stretches = lax.axis_size("dp"), lax.axis_size("seq")
    norming = 1.0 / math.sqrt(copies * hidden.shape[0] * hidden.shape[1] * stretches)
    device = packed_device if (copies, stretches) == (2, 16) else plain_device
    return device(hidden, letters, gate_input, cotangent, embedding, filter_taps, norming)


def solution(mesh):
    return jax.shard_map(
        per_device,
        mesh=mesh,
        in_specs=(
            P("dp", "seq", None),
            P("dp", "seq"),
            P("dp", "seq", None),
            P("dp", "seq", None),
            P(),
            P(None, "seq", None),
        ),
        out_specs=(
            P("dp", "seq", None),
            P("dp", "seq", None),
            P("dp", "seq", None),
            P(None, "seq", None),
            P(),
        ),
        check_vma=False,
    )
```

```python
import math

import jax
import jax.numpy as jnp
import numpy as np
from jax import lax
from jax.experimental import pallas as pl
from jax.experimental.pallas import tpu as pltpu
from jax.sharding import PartitionSpec as P

BLOCK = 512
COLS = 256
LANES = 128
STEP = 16
CHUNK = 128
HALF_ROOT = 0.5**0.5
CHUNK_ROWS = 74

F32 = jnp.float32
BF16 = jnp.bfloat16


def tables():
    index = np.arange(CHUNK)[:, None]
    forward, backward = [], []
    for step, first, inputs in ((4, 0, 2), (4, 2, 2), (8, 1, 1), (8, 5, 1)):
        moment = np.arange(CHUNK * inputs)[None, :]
        phases = (step * index + first) * moment % (2 * BLOCK)
        angles = phases * (np.pi / BLOCK)
        cosines, sines = np.cos(angles), np.sin(angles)
        if inputs == 2:
            lower = -sines
            if first == 0:
                lower[0] = 1.0 - 2.0 * (moment[0] % 2)
            table = np.concatenate([cosines, lower], axis=0)
        else:
            upper = np.concatenate([cosines, sines], axis=1)
            table = np.concatenate([upper, np.concatenate([-sines, cosines], axis=1)], axis=0)
        weights = np.full((2 * CHUNK, 1), 1.0 / BLOCK)
        if first == 0:
            weights[0] = weights[CHUNK] = 0.5 / BLOCK
        forward.append(table)
        backward.append((table * weights).T)

    def halves(parts):
        table = np.concatenate(parts, axis=0)
        high = table.astype(jnp.bfloat16)
        return high, (table - high.astype(np.float64)).astype(jnp.bfloat16)

    return (*halves(forward), *halves(backward))


def iota(shape, axis):
    return lax.broadcasted_iota(jnp.int32, shape, axis)


def matmul(left, right):
    return jnp.dot(left, right, preferred_element_type=F32)


def turn(array, quarters):
    if isinstance(quarters, int) and quarters % 4 == 0:
        return array
    return pltpu.roll(array, 32 * (quarters & 3), 1)


def choose(arrays, offset, shift):
    block = ((iota(arrays[0].shape, 1) >> 5) - shift) & 3
    result = arrays[0]
    for index in range(1, 4):
        result = jnp.where(block == (index + offset) % 4, arrays[index], result)
    return result


def spread(rows, shift):
    turned = [turn(array, q + shift) for q, array in enumerate(rows)]
    return [choose(turned, d, shift) for d in range(4)]


def collect(chunks, shift):
    return [turn(choose(chunks, q, shift), -q - shift) for q in range(4)]


def owner_shift():
    return lax.axis_index("seq") & 3


def stretch_shift():
    return 2 * ((lax.axis_index("seq") >> 2) & 1) + lax.axis_index("dp")


def channel_source(lane):
    group, spot = lane >> 5, lane & 31
    return jnp.where(spot < 16, 16 * group + spot, 271 - 16 * group - spot)


def gather_channels():
    row, lane = iota((256, 256), 0), iota((1, 256), 1)
    return jnp.where(row == channel_source(lane), 1.0, 0.0).astype(BF16)


def return_channels():
    row, lane = iota((256, 1), 0), iota((256, 256), 1)
    return jnp.where(channel_source(row) == lane, 1.0, 0.0).astype(BF16)


def copy_in(pairs, sems):
    copies = [pltpu.make_async_copy(source, target, sems.at[index]) for index, (source, target) in enumerate(pairs)]
    for copy in copies:
        copy.start()
    return copies


def gathered_rows(part, gather):
    columns = []
    for u in range(4):
        pair = jnp.concatenate([part[:, 128 * u : 128 * u + 128], part[:, 896 - 128 * u : 1024 - 128 * u]], axis=1)
        both = matmul(pair, gather)
        columns += [both[:, :LANES], both[:, LANES:]]
    return columns


def send_stretch(part, gather, send_ref, place):
    shift = stretch_shift()
    for m, block in enumerate(gathered_rows(part, gather)):
        for d, chunk in enumerate(spread([block[32 * q : 32 * q + 32] for q in range(4)], shift)):
            send_ref[4 * m + d, place : place + 32, :] = chunk.astype(BF16)


def pack_kernel(
    hidden_hbm, letters_hbm, gate_hbm, upstream_hbm, embedding_hbm, taps_hbm, send_ref,
    hidden_ref, letters_ref, gate_ref, upstream_ref, embedding_ref, taps_ref, sems,
):
    copies = copy_in(
        [
            (letters_hbm, letters_ref),
            (embedding_hbm, embedding_ref),
            (hidden_hbm, hidden_ref),
            (gate_hbm, gate_ref),
            (upstream_hbm, upstream_ref),
            (taps_hbm.at[pl.ds(2 * lax.axis_index("dp"), 2)], taps_ref),
        ],
        sems,
    )
    gather = gather_channels()
    for copy in copies:
        copy.wait()
    letters = letters_ref[...].astype(F32)
    square = iota((128, 128), 0) == iota((128, 128), 1)
    letter = jnp.sum(jnp.where(square, letters, 0.0), axis=1, keepdims=True)
    added = embedding_ref[0:1, :]
    for index in range(1, 4):
        added = jnp.where(letter == float(index), embedding_ref[index : index + 1, :], added)
    send_stretch((hidden_ref[0].astype(F32) + added).astype(BF16), gather, send_ref, 0)
    send_stretch((upstream_ref[0].astype(F32) * gate_ref[0].astype(F32)).astype(BF16), gather, send_ref, 32)
    rows = gathered_rows(taps_ref[...].astype(F32).reshape(16, 1024).astype(BF16), gather)
    line = jnp.broadcast_to(letters, (8, 128))
    which, lane = iota((8, 128), 0), iota((8, 128), 1)
    shown = jnp.where(which == 0, pltpu.roll(line, 64, 1), jnp.where(which == 1, line, 0.0))
    for m, block in enumerate(rows):
        for d in range(4):
            first = turn(block[0:8], (4 - d) % 4)
            second = turn(block[8:16], (5 - d) % 4)
            piece = jnp.where(lane >= 64, shown, jnp.where(lane >= 32, second, first))
            send_ref[4 * m + d, 64:72, :] = piece.astype(BF16)


def load_pair(ref, base, start, size):
    return tuple(
        [ref[row : row + STEP, lane : lane + LANES] for lane in range(start, start + size, LANES)]
        for row in (base, base + CHUNK)
    )


def with_neighbours(pair, width, odd):
    lane = iota((STEP, LANES), 1)

    def added(here, there):
        return here - there if odd else here + there

    if width == LANES // 2:
        back, on = [], []
        for first, second in pair:
            turned, other = pltpu.roll(first, width, 1), pltpu.roll(second, width, 1)
            between = jnp.where(lane < width, turned, other)
            back.append([added(first, jnp.where(lane < width, 0.0, turned)), added(second, between)])
            on.append([added(first, between), added(second, jnp.where(lane < width, other, 0.0))])
        return tuple(back), tuple(on)
    lane = iota((STEP, COLS), 1)
    both = []
    for shift, keep in ((width, lane >= width), (COLS - width, lane < COLS - width)):
        moved = []
        for parts in pair:
            wide = jnp.concatenate(parts, axis=1)
            wide = added(wide, jnp.where(keep, pltpu.roll(wide, shift, 1), 0.0))
            moved.append([wide[:, :LANES], wide[:, LANES:]])
        both.append(tuple(moved))
    return tuple(both)


def products(first):
    real_row = iota((STEP, LANES), 0) == 0

    def settle(a, b, real, imaginary):
        if first:
            real = jnp.where(real_row, a[0] * b[0], real)
            imaginary = jnp.where(real_row, a[1] * b[1], imaginary)
        return real, imaginary

    def times(a, b):
        return settle(a, b, a[0] * b[0] - a[1] * b[1], a[0] * b[1] + a[1] * b[0])

    def times_conjugate(a, b):
        return settle(a, b, a[0] * b[0] + a[1] * b[1], a[1] * b[0] - a[0] * b[1])

    return times, times_conjugate


def plus(a, b):
    return a[0] + b[0], a[1] + b[1]


def column(pair, index):
    return pair[0][index], pair[1][index]


def store_split(high_ref, low_ref, base, start, pair):
    for row, part in ((base, 0), (base + CHUNK, 1)):
        high = pair[part].astype(BF16)
        high_ref[row : row + STEP, start : start + LANES] = high
        low_ref[row : row + STEP, start : start + LANES] = (pair[part] - high.astype(F32)).astype(BF16)


def spectra_step(spectra_ref, high_ref, low_ref, narrow, width, base):
    times, times_conjugate = products(base == 0)
    odd = base >= 4 * CHUNK
    back, on = with_neighbours(load_pair(spectra_ref, base, 0, COLS), width, odd)
    own = column(load_pair(spectra_ref, base, 2 * COLS, LANES), 0)
    mirror = column(load_pair(spectra_ref, base, 2 * COLS + LANES, LANES), 0)
    for index in range(2):
        field = plus(times(column(back, index), own), times_conjugate(column(on, index), mirror))
        store_split(high_ref, low_ref, base, LANES * index, field)
    grads = load_pair(spectra_ref, base, COLS, COLS)
    causal, ahead = None, None
    for index in range(2):
        one = times_conjugate(column(grads, index), column(back, index))
        two = times_conjugate(column(on, index), column(grads, index))
        causal = one if causal is None else plus(causal, one)
        ahead = two if ahead is None else plus(ahead, two)
    lags = plus(causal, tuple(pltpu.roll(part, narrow // 2, 1) for part in ahead))
    for row, part in ((base, lags[0]), (base + CHUNK, lags[1])):
        high = part.astype(BF16)
        high_ref[row : row + STEP, 2 * COLS : 2 * COLS + LANES] = high
        high_ref[row : row + STEP, 2 * COLS + LANES : 3 * COLS] = (part - high.astype(F32)).astype(BF16)
    back, on = with_neighbours(grads, width, odd)
    for index in range(2):
        wanted = plus(times(column(back, index), mirror), times_conjugate(column(on, index), own))
        store_split(high_ref, low_ref, base, COLS + LANES * index, wanted)


def fold(quarters):
    one, two, three, four = quarters
    between, both = HALF_ROOT * (two - four), HALF_ROOT * (two + four)
    return [one + three, two + four, one - three, two - four, one + between, -three - both, one - between, both - three]


def unfold(parts):
    between, both = HALF_ROOT * (parts[4] - parts[6]), HALF_ROOT * (parts[5] - parts[7])
    one, two = parts[0] + parts[2], parts[1] + parts[3]
    three, four = parts[0] - parts[2], parts[1] - parts[3]
    return [
        one + (parts[4] + parts[6]),
        two + (between - both),
        three - (parts[5] + parts[7]),
        four - (between + both),
    ]


def store_folded(high_ref, low_ref, row, lane, quarters):
    rows, lanes = quarters[0].shape
    for index, part in enumerate(fold(quarters)):
        start = CHUNK * index + row
        high = part.astype(BF16)
        high_ref[start : start + rows, lane : lane + lanes] = high
        low_ref[start : start + rows, lane : lane + lanes] = (part - high.astype(F32)).astype(BF16)


def transforms(inputs, table_refs, spectra_ref, high_ref, low_ref, classes_ref, result_ref, narrow, width):
    inputs_high, inputs_low = inputs
    forward_high, forward_low, backward_high, backward_low = table_refs
    chunks = BLOCK // CHUNK

    def rows_of(chunk):
        return slice(2 * CHUNK * chunk, 2 * CHUNK * (chunk + 1))

    def forward(chunk, start):
        rows = rows_of(chunk)
        columns = slice(start, start + COLS)
        spectra_ref[rows, columns] = (
            matmul(forward_high[rows, :], inputs_high[rows, columns])
            + matmul(forward_low[rows, :], inputs_high[rows, columns])
            + matmul(forward_high[rows, :], inputs_low[rows, columns])
        )

    def backward(chunk):
        rows = rows_of(chunk)
        for start in (COLS, 2 * COLS, 0):
            columns = slice(start, start + COLS)
            made = matmul(backward_high[rows, :], high_ref[rows, columns]) + matmul(
                backward_low[rows, :], high_ref[rows, columns]
            )
            if start < 2 * COLS:
                classes_ref[rows, columns] = made + matmul(backward_high[rows, :], low_ref[rows, columns])
            else:
                classes_ref[rows, start : start + LANES] = made[:, :LANES] + made[:, LANES:]

    for start in (2 * COLS, 0, COLS):
        for chunk in range(chunks):
            forward(chunk, start)
    for chunk in range(chunks):
        for base in range(2 * CHUNK * chunk, 2 * CHUNK * chunk + CHUNK, STEP):
            spectra_step(spectra_ref, high_ref, low_ref, narrow, width, base)
        backward(chunk)
    for lane in (COLS, COLS + LANES, 2 * COLS, 0, LANES):
        lanes = slice(lane, lane + LANES)
        for row in range(0, CHUNK, 32):
            parts = [classes_ref[CHUNK * index + row : CHUNK * index + row + 32, lanes] for index in range(8)]
            for quarter, part in enumerate(unfold(parts)):
                result_ref[CHUNK * quarter + row : CHUNK * quarter + row + 32, lanes] = part


def column_sum(total, narrow):
    shift = LANES // 2
    while shift >= narrow:
        total = total + pltpu.roll(total, shift, 1)
        shift //= 2
    return total


def letter_sums(values_grad, choice, belongs, narrow):
    high = values_grad.astype(BF16)
    low = (values_grad - high.astype(F32)).astype(BF16)
    sums = jnp.where(belongs, matmul(choice, high) + matmul(choice, low), 0.0)
    groups = sums.shape[0] // 4
    rows = [jnp.sum(sums[groups * a : groups * a + groups], axis=0, keepdims=True) for a in range(4)]
    total = jnp.concatenate(rows, axis=0)
    return column_sum(total[:, :LANES] + total[:, LANES:], narrow)


PLACES = [(u, s) for u in range(2) for s in range(4)]


def unpack_block(receive_ref, place, high_ref, low_ref, lanes):
    shift = owner_shift()
    for u in range(2):
        stretches = []
        for s in range(4):
            chunks = [
                receive_ref[16 * d + 4 * (2 * u + j) + s, place : place + 32, :].astype(F32)
                for j in range(2)
                for d in range(2)
            ]
            stretches.append(collect(chunks, shift))
        for q in range(4):
            store_folded(high_ref, low_ref, 32 * q, lanes + 128 * u, [rows[q] for rows in stretches])


def put(send_ref, index, pair, rows):
    start = CHUNK_ROWS * index + 2 * pair
    send_ref[start : start + rows.shape[0], :] = rows.astype(BF16)


def take(receive_ref, index, pair, count):
    return receive_ref[index, pair : pair + count].reshape(2 * count, LANES).astype(F32)


def pack_block(result_ref, lanes, send_ref, pair):
    shift = owner_shift()
    for u, s in PLACES:
        rows = [
            result_ref[128 * s + 32 * q : 128 * s + 32 * q + 32, lanes + 128 * u : lanes + 128 * u + 128]
            for q in range(4)
        ]
        for group, chunk in enumerate(spread(rows, shift)):
            j, d = group // 2, group % 2
            put(send_ref, 16 * d + 4 * (2 * u + j) + s, pair, chunk)


def unpack_taps(tails, high_ref, low_ref):
    row, lane = iota((128, 256), 0), iota((1, 256), 1)
    spot = (lane & 31) ^ ((lane >> 7) << 4)
    quarters = []
    for d in range(2):
        tail = tails[16 * d : 16 * d + 16].reshape(128, 128).astype(BF16)
        for k in range(2):
            quarters.append(matmul(tail, jnp.where(row == 32 * k + spot, 1.0, 0.0).astype(BF16)))
    store_folded(high_ref, low_ref, 0, 512, quarters)


def pack_tails(norming, tails, result_ref, send_ref):
    quarter = ((iota((128, 128), 1) >> 5) - lax.axis_index("seq")) & 3
    sums = column_sum(result_ref[:, 512:640], 32)
    lags = sums[0:128]
    for k in range(1, 4):
        lags = jnp.where(quarter == k, sums[128 * k : 128 * k + 128], lags)
    lags = lags * norming
    for index in range(16):
        put(send_ref, index, 32, lags[8 * index : 8 * index + 8])
        put(send_ref, 16 + index, 32, lags[8 * index : 8 * index + 8])
    line, source = iota((32, 128), 1), iota((32, 128), 0)
    letters = jnp.where(line < 64, pltpu.roll(tails[:, 0, :], 64, 1), tails[:, 1, :])
    choice = []
    for a in range(4):
        chosen = jnp.where(letters == float(a), 1.0, 0.0)
        choice.append(jnp.concatenate([jnp.where((source & 3) == s, chosen, 0.0) for s in range(4)], axis=1))
    choice = jnp.concatenate(choice, axis=0).astype(BF16)
    source = iota((128, 256), 0) & 31
    belongs = (((source >> 2) & 3) * 2 + (source >> 4)) == (iota((128, 256), 1) >> 5)
    sums = letter_sums(result_ref[:, 256:512], choice, belongs, 32) * norming
    sums = choose([sums[a : a + 1] for a in range(4)], 0, owner_shift())
    high = sums.astype(BF16).astype(F32)
    tile = jnp.concatenate([high, sums - high], axis=0)
    for index in range(32):
        put(send_ref, index, 36, tile)


def middle_kernel(
    norming, receive_ref, fh_ref, fl_ref, bh_ref, bl_ref, send_ref,
    inputs_high_ref, inputs_low_ref, spectra_ref, high_ref, low_ref, classes_ref, result_ref,
):
    tails = receive_ref[:, 64:72, :].astype(F32)
    unpack_taps(tails, inputs_high_ref, inputs_low_ref)
    unpack_block(receive_ref, 0, inputs_high_ref, inputs_low_ref, 0)
    unpack_block(receive_ref, 32, inputs_high_ref, inputs_low_ref, 256)
    transforms(
        (inputs_high_ref, inputs_low_ref), (fh_ref, fl_ref, bh_ref, bl_ref),
        spectra_ref, high_ref, low_ref, classes_ref, result_ref, 32, 64,
    )
    pack_tails(norming, tails, result_ref, send_ref)
    pack_block(result_ref, 256, send_ref, 16)
    pack_block(result_ref, 0, send_ref, 0)


def received_columns(receive_ref, pair, back):
    shift = stretch_shift()
    result = []
    for u in range(4):
        columns = []
        for m in (2 * u, 2 * u + 1):
            chunks = [take(receive_ref, 4 * m + d, pair, 16) for d in range(4)]
            columns.append(jnp.concatenate(collect(chunks, shift), axis=0).astype(BF16))
        result.append(matmul(jnp.concatenate(columns, axis=1), back))
    return result


def places_of(u):
    return ((slice(128 * u, 128 * u + 128), slice(0, 128)), (slice(896 - 128 * u, 1024 - 128 * u), slice(128, 256)))


def finish_kernel(receive_ref, gate_ref, upstream_ref, out_ref, hidden_ref, gated_ref, filter_ref, embedding_ref):
    back = return_channels()
    for u, field in enumerate(received_columns(receive_ref, 0, back)):
        for there, here in places_of(u):
            out_ref[0, :, there] = (gate_ref[0, :, there].astype(F32) * field[:, here]).astype(BF16)
            gated_ref[0, :, there] = (upstream_ref[0, :, there].astype(F32) * field[:, here]).astype(BF16)
    for u, rows in enumerate(received_columns(receive_ref, 16, back)):
        for there, here in places_of(u):
            hidden_ref[0, :, there] = rows[:, here].astype(BF16)
    for u in range(4):
        columns = []
        for m in (2 * u, 2 * u + 1):
            columns.append(jnp.concatenate(collect([take(receive_ref, 4 * m + d, 32, 4) for d in range(4)], 0), axis=0))
        done = matmul(jnp.concatenate(columns, axis=1).astype(BF16), back)
        for there, here in places_of(u):
            filter_ref[:, :, there] = done[:, here].reshape(4, 8, 128)
    sums = collect(
        [jnp.concatenate([take(receive_ref, 4 * m + d, 36, 1) for m in range(8)], axis=0) for d in range(4)], 0
    )
    rows = []
    for term in range(2):
        for u in range(4):
            for total in sums:
                first, second = total[4 * u + term : 4 * u + term + 1], total[4 * u + 2 + term : 4 * u + 3 + term]
                rows.append(jnp.concatenate([first, second], axis=1))
    done = matmul(jnp.concatenate(rows, axis=0).astype(BF16), back)
    done = done[0:16] + done[16:32]
    for u in range(4):
        for there, here in places_of(u):
            embedding_ref[:, there] = done[4 * u : 4 * u + 4, here]


WORK = [
    pltpu.VMEM((2 * BLOCK, 3 * COLS), BF16),
    pltpu.VMEM((2 * BLOCK, 3 * COLS), BF16),
    pltpu.VMEM((2 * BLOCK, 3 * COLS), F32),
    pltpu.VMEM((2 * BLOCK, 3 * COLS), BF16),
    pltpu.VMEM((2 * BLOCK, 2 * COLS), BF16),
    pltpu.VMEM((2 * BLOCK, 2 * COLS + LANES), F32),
    pltpu.VMEM((BLOCK, 2 * COLS + LANES), F32),
]
VM = pl.BlockSpec(memory_space=pltpu.VMEM)
HBM = pl.BlockSpec(memory_space=pltpu.HBM)


def shape_of(*dims, dtype=BF16):
    return jax.ShapeDtypeStruct(dims, dtype)


def call(kernel, specs, shapes, scratch=(), mebibytes=32):
    return pl.pallas_call(
        kernel,
        in_specs=specs,
        out_shape=shapes,
        scratch_shapes=scratch,
        compiler_params=pltpu.CompilerParams(vmem_limit_bytes=mebibytes * 1024 * 1024),
    )


def in_hbm(array):
    return pltpu.with_memory_space_constraint(array, pltpu.HBM)


def exchange(array):
    return lax.all_to_all(array, ("dp", "seq"), 0, 0, tiled=True)


def packed_device(hidden, letters, gate_input, cotangent, embedding, filter_taps, norming):
    stretch = pltpu.VMEM(hidden.shape, BF16)
    sent = call(
        pack_kernel,
        [HBM] * 6,
        shape_of(32, 72, 128),
        [
            stretch,
            pltpu.VMEM(letters.shape, jnp.int32),
            stretch,
            stretch,
            pltpu.VMEM(embedding.shape, F32),
            pltpu.VMEM((2, 8, 1024), BF16),
            pltpu.SemaphoreType.DMA((6,)),
        ],
        16,
    )(*(in_hbm(array) for array in (hidden, letters, gate_input, cotangent, embedding, filter_taps)))
    here = exchange(sent)
    def kernel(*refs):
        middle_kernel(norming, *refs)

    sent = call(
        kernel,
        [VM] * 5,
        shape_of(32 * CHUNK_ROWS, LANES),
        WORK,
        24,
    )(here, *tables())
    here = exchange(sent.reshape(32, CHUNK_ROWS // 2, 2, LANES))
    shape = jax.ShapeDtypeStruct(hidden.shape, BF16)
    return call(
        finish_kernel,
        [VM] * 3,
        (shape, shape, shape, shape_of(*filter_taps.shape, dtype=F32), shape_of(*embedding.shape, dtype=F32)),
        (),
        16,
    )(here, gate_input, cotangent)


def plain_kernel(
    narrow, width, letters_ref, samples_ref, fh_ref, fl_ref, bh_ref, bl_ref, field_ref, back_ref, lags_ref, sums_ref,
    inputs_high_ref, inputs_low_ref, spectra_ref, high_ref, low_ref, classes_ref, result_ref,
):
    for lane in range(0, 3 * COLS, LANES):
        quarters = [samples_ref[row : row + CHUNK, lane : lane + LANES].astype(F32) for row in range(0, BLOCK, CHUNK)]
        store_folded(inputs_high_ref, inputs_low_ref, 0, lane, quarters)
    transforms(
        (inputs_high_ref, inputs_low_ref), (fh_ref, fl_ref, bh_ref, bl_ref),
        spectra_ref, high_ref, low_ref, classes_ref, result_ref, narrow, width,
    )
    field_ref[...] = result_ref[:, 0:COLS].astype(BF16)
    back_ref[...] = result_ref[:, COLS : 2 * COLS].astype(BF16)
    lags_ref[...] = column_sum(result_ref[:, 2 * COLS :], narrow)
    letters = letters_ref[...]
    groups = COLS // narrow
    choice = jnp.concatenate(
        [jnp.where(letters == float(a), 1.0, 0.0) for a in range(4)], axis=0
    ).astype(BF16)
    shape = (4 * groups, COLS)
    belongs = (iota(shape, 0) & (groups - 1)) == iota(shape, 1) // narrow
    sums_ref[...] = letter_sums(result_ref[:, COLS : 2 * COLS], choice, belongs, narrow)


def plain_device(hidden, letters, gate_input, cotangent, embedding, filter_taps, norming):
    axes = ("dp", "seq")
    copies, stretches = lax.axis_size("dp"), lax.axis_size("seq")
    devices = copies * stretches
    stretch, channels = hidden.shape[1], hidden.shape[2]
    narrow = channels // devices
    half = narrow // 2
    blocks = stretch * stretches // BLOCK
    low = np.arange(channels // 2).reshape(devices, half)
    order = np.concatenate([low, channels - 1 - low], axis=1).reshape(-1)
    restore = np.argsort(order)
    onehot = (letters[0][:, None] == jnp.arange(embedding.shape[0], dtype=jnp.int32)[None, :]).astype(F32)
    added = jnp.dot(onehot, embedding, precision=lax.Precision.HIGHEST)
    values = (hidden[0].astype(F32) + added).astype(BF16)
    gate_wide, upstream = gate_input[0].astype(F32), cotangent[0].astype(F32)
    field_grad = (upstream * gate_wide).astype(BF16)

    def scatter(array):
        parts = jnp.take(array, order, axis=1).reshape(stretch, devices, narrow).swapaxes(0, 1)
        parts = lax.all_to_all(parts, axes, 0, 0, tiled=True)
        parts = parts.reshape(copies, blocks, BLOCK, narrow)
        return parts.transpose(2, 1, 0, 3).reshape(BLOCK, COLS)

    def gather(columns):
        parts = columns.reshape(BLOCK, blocks, copies, narrow).transpose(2, 1, 0, 3)
        parts = parts.reshape(devices, stretch, narrow)
        parts = lax.all_to_all(parts, axes, 0, 0, tiled=True)
        return jnp.take(parts.swapaxes(0, 1).reshape(stretch, channels), restore, axis=1)

    taps = lax.all_gather(filter_taps, "seq", axis=1, tiled=True).reshape(BLOCK, channels)
    mine = lax.axis_index("dp") * stretches + lax.axis_index("seq")
    own = lax.dynamic_slice_in_dim(jnp.take(taps, order, axis=1), mine * narrow, narrow, axis=1)
    mirror = jnp.roll(own, half, axis=1)
    repeats = LANES // narrow
    samples = jnp.concatenate(
        [scatter(values), scatter(field_grad), jnp.tile(own, (1, repeats)), jnp.tile(mirror, (1, repeats))], axis=1
    )
    marks = lax.all_gather(letters[0].astype(F32), axes, tiled=True)
    marks = marks.reshape(copies, blocks, BLOCK).swapaxes(0, 1).reshape(copies * blocks, BLOCK)

    def kernel(*refs):
        plain_kernel(narrow, copies * narrow, *refs)

    field, back, lags, sums = call(
        kernel,
        [VM] * 6,
        (
            shape_of(BLOCK, COLS),
            shape_of(BLOCK, COLS),
            shape_of(BLOCK, LANES, dtype=F32),
            shape_of(embedding.shape[0], LANES, dtype=F32),
        ),
        WORK,
    )(marks, samples, *tables())
    small = jnp.concatenate([lags[:, :narrow], sums[:, :narrow]], axis=0) * norming
    small = jnp.take(lax.all_gather(small, axes, axis=1, tiled=True), restore, axis=1)
    rows = filter_taps.shape[1]
    filter_grad = lax.dynamic_slice_in_dim(
        small[:BLOCK].reshape(filter_taps.shape[0], stretch, channels), lax.axis_index("seq") * rows, rows, axis=1
    )
    field_rows, grad_rows = gather(field).astype(F32), gather(back)
    output = (gate_wide * field_rows).astype(BF16)[None]
    gate_grad = (upstream * field_rows).astype(BF16)[None]
    return output, grad_rows[None], gate_grad, filter_grad, small[BLOCK:]


def per_device(hidden, letters, gate_input, cotangent, embedding, filter_taps):
    copies, stretches = lax.axis_size("dp"), lax.axis_size("seq")
    norming = 1.0 / math.sqrt(copies * hidden.shape[0] * hidden.shape[1] * stretches)
    device = packed_device if (copies, stretches) == (2, 16) else plain_device
    return device(hidden, letters, gate_input, cotangent, embedding, filter_taps, norming)


def solution(mesh):
    return jax.shard_map(
        per_device,
        mesh=mesh,
        in_specs=(
            P("dp", "seq", None),
            P("dp", "seq"),
            P("dp", "seq", None),
            P("dp", "seq", None),
            P(),
            P(None, "seq", None),
        ),
        out_specs=(
            P("dp", "seq", None),
            P("dp", "seq", None),
            P("dp", "seq", None),
            P(None, "seq", None),
            P(),
        ),
        check_vma=False,
    )
```

```python
import math

import jax
import jax.numpy as jnp
import numpy as np
from jax import lax
from jax.experimental import pallas as pl
from jax.experimental.pallas import tpu as pltpu
from jax.sharding import PartitionSpec as P

BLOCK = 512
COLS = 256
LANES = 128
STEP = 16
CHUNK = 128
HALF_ROOT = 0.5**0.5
CHUNK_ROWS = 74

F32 = jnp.float32
BF16 = jnp.bfloat16


def tables():
    index = np.arange(CHUNK)[:, None]
    forward, backward = [], []
    for step, first, inputs in ((4, 0, 2), (4, 2, 2), (8, 1, 1), (8, 5, 1)):
        moment = np.arange(CHUNK * inputs)[None, :]
        phases = (step * index + first) * moment % (2 * BLOCK)
        angles = phases * (np.pi / BLOCK)
        cosines, sines = np.cos(angles), np.sin(angles)
        if inputs == 2:
            lower = -sines
            if first == 0:
                lower[0] = 1.0 - 2.0 * (moment[0] % 2)
            table = np.concatenate([cosines, lower], axis=0)
        else:
            upper = np.concatenate([cosines, sines], axis=1)
            table = np.concatenate([upper, np.concatenate([-sines, cosines], axis=1)], axis=0)
        weights = np.full((2 * CHUNK, 1), 1.0 / BLOCK)
        if first == 0:
            weights[0] = weights[CHUNK] = 0.5 / BLOCK
        forward.append(table)
        backward.append((table * weights).T)

    def halves(parts):
        table = np.concatenate(parts, axis=0)
        high = table.astype(jnp.bfloat16)
        return high, (table - high.astype(np.float64)).astype(jnp.bfloat16)

    return (*halves(forward), *halves(backward))


def iota(shape, axis):
    return lax.broadcasted_iota(jnp.int32, shape, axis)


def matmul(left, right):
    return jnp.dot(left, right, preferred_element_type=F32)


def turn(array, quarters):
    if isinstance(quarters, int) and quarters % 4 == 0:
        return array
    return pltpu.roll(array, 32 * (quarters & 3), 1)


def choose(arrays, offset, shift):
    block = ((iota(arrays[0].shape, 1) >> 5) - shift) & 3
    result = arrays[0]
    for index in range(1, 4):
        result = jnp.where(block == (index + offset) % 4, arrays[index], result)
    return result


def spread(rows, shift):
    turned = [turn(array, q + shift) for q, array in enumerate(rows)]
    return [choose(turned, d, shift) for d in range(4)]


def collect(chunks, shift):
    return [turn(choose(chunks, q, shift), -q - shift) for q in range(4)]


def owner_shift():
    return lax.axis_index("seq") & 3


def stretch_shift():
    return 2 * ((lax.axis_index("seq") >> 2) & 1) + lax.axis_index("dp")


def channel_source(lane):
    group, spot = lane >> 5, lane & 31
    return jnp.where(spot < 16, 16 * group + spot, 271 - 16 * group - spot)


def gather_channels():
    row, lane = iota((256, 256), 0), iota((1, 256), 1)
    return jnp.where(row == channel_source(lane), 1.0, 0.0).astype(BF16)


def return_channels():
    row, lane = iota((256, 1), 0), iota((256, 256), 1)
    return jnp.where(channel_source(row) == lane, 1.0, 0.0).astype(BF16)


def copy_in(pairs, sems):
    copies = [pltpu.make_async_copy(source, target, sems.at[index]) for index, (source, target) in enumerate(pairs)]
    for copy in copies:
        copy.start()
    return copies


def gathered_rows(part, gather):
    columns = []
    for u in range(4):
        pair = jnp.concatenate([part[:, 128 * u : 128 * u + 128], part[:, 896 - 128 * u : 1024 - 128 * u]], axis=1)
        both = matmul(pair, gather)
        columns += [both[:, :LANES], both[:, LANES:]]
    return columns


def send_stretch(part, gather, send_ref, place):
    shift = stretch_shift()
    for m, block in enumerate(gathered_rows(part, gather)):
        for d, chunk in enumerate(spread([block[32 * q : 32 * q + 32] for q in range(4)], shift)):
            send_ref[4 * m + d, place : place + 32, :] = chunk.astype(BF16)


def pack_kernel(
    hidden_hbm, letters_hbm, gate_hbm, upstream_hbm, embedding_hbm, taps_hbm, send_ref,
    hidden_ref, letters_ref, gate_ref, upstream_ref, embedding_ref, taps_ref, sems,
):
    copies = copy_in(
        [
            (letters_hbm, letters_ref),
            (embedding_hbm, embedding_ref),
            (hidden_hbm, hidden_ref),
            (gate_hbm, gate_ref),
            (upstream_hbm, upstream_ref),
            (taps_hbm.at[pl.ds(2 * lax.axis_index("dp"), 2)], taps_ref),
        ],
        sems,
    )
    gather = gather_channels()
    for copy in copies:
        copy.wait()
    letters = letters_ref[...].astype(F32)
    square = iota((128, 128), 0) == iota((128, 128), 1)
    letter = jnp.sum(jnp.where(square, letters, 0.0), axis=1, keepdims=True)
    added = embedding_ref[0:1, :]
    for index in range(1, 4):
        added = jnp.where(letter == float(index), embedding_ref[index : index + 1, :], added)
    send_stretch((hidden_ref[0].astype(F32) + added).astype(BF16), gather, send_ref, 0)
    send_stretch((upstream_ref[0].astype(F32) * gate_ref[0].astype(F32)).astype(BF16), gather, send_ref, 32)
    rows = gathered_rows(taps_ref[...].astype(F32).reshape(16, 1024).astype(BF16), gather)
    line = jnp.broadcast_to(letters, (8, 128))
    which, lane = iota((8, 128), 0), iota((8, 128), 1)
    shown = jnp.where(which == 0, pltpu.roll(line, 64, 1), jnp.where(which == 1, line, 0.0))
    for m, block in enumerate(rows):
        for d in range(4):
            first = turn(block[0:8], (4 - d) % 4)
            second = turn(block[8:16], (5 - d) % 4)
            piece = jnp.where(lane >= 64, shown, jnp.where(lane >= 32, second, first))
            send_ref[4 * m + d, 64:72, :] = piece.astype(BF16)


def load_pair(ref, base, start, size):
    return tuple(
        [ref[row : row + STEP, lane : lane + LANES] for lane in range(start, start + size, LANES)]
        for row in (base, base + CHUNK)
    )


def with_neighbours(pair, width, odd):
    lane = iota((STEP, LANES), 1)

    def added(here, there):
        return here - there if odd else here + there

    if width == LANES // 2:
        back, on = [], []
        for first, second in pair:
            turned, other = pltpu.roll(first, width, 1), pltpu.roll(second, width, 1)
            between = jnp.where(lane < width, turned, other)
            back.append([added(first, jnp.where(lane < width, 0.0, turned)), added(second, between)])
            on.append([added(first, between), added(second, jnp.where(lane < width, other, 0.0))])
        return tuple(back), tuple(on)
    lane = iota((STEP, COLS), 1)
    both = []
    for shift, keep in ((width, lane >= width), (COLS - width, lane < COLS - width)):
        moved = []
        for parts in pair:
            wide = jnp.concatenate(parts, axis=1)
            wide = added(wide, jnp.where(keep, pltpu.roll(wide, shift, 1), 0.0))
            moved.append([wide[:, :LANES], wide[:, LANES:]])
        both.append(tuple(moved))
    return tuple(both)


def products(first):
    real_row = iota((STEP, LANES), 0) == 0

    def settle(a, b, real, imaginary):
        if first:
            real = jnp.where(real_row, a[0] * b[0], real)
            imaginary = jnp.where(real_row, a[1] * b[1], imaginary)
        return real, imaginary

    def times(a, b):
        return settle(a, b, a[0] * b[0] - a[1] * b[1], a[0] * b[1] + a[1] * b[0])

    def times_conjugate(a, b):
        return settle(a, b, a[0] * b[0] + a[1] * b[1], a[1] * b[0] - a[0] * b[1])

    return times, times_conjugate


def plus(a, b):
    return a[0] + b[0], a[1] + b[1]


def column(pair, index):
    return pair[0][index], pair[1][index]


def store_split(high_ref, low_ref, base, start, pair):
    for row, part in ((base, 0), (base + CHUNK, 1)):
        high = pair[part].astype(BF16)
        high_ref[row : row + STEP, start : start + LANES] = high
        low_ref[row : row + STEP, start : start + LANES] = (pair[part] - high.astype(F32)).astype(BF16)


def spectra_step(spectra_ref, high_ref, low_ref, narrow, width, base):
    times, times_conjugate = products(base == 0)
    odd = base >= 4 * CHUNK
    back, on = with_neighbours(load_pair(spectra_ref, base, 0, COLS), width, odd)
    own = column(load_pair(spectra_ref, base, 2 * COLS, LANES), 0)
    mirror = column(load_pair(spectra_ref, base, 2 * COLS + LANES, LANES), 0)
    for index in range(2):
        field = plus(times(column(back, index), own), times_conjugate(column(on, index), mirror))
        store_split(high_ref, low_ref, base, LANES * index, field)
    grads = load_pair(spectra_ref, base, COLS, COLS)
    causal, ahead = None, None
    for index in range(2):
        one = times_conjugate(column(grads, index), column(back, index))
        two = times_conjugate(column(on, index), column(grads, index))
        causal = one if causal is None else plus(causal, one)
        ahead = two if ahead is None else plus(ahead, two)
    lags = plus(causal, tuple(pltpu.roll(part, narrow // 2, 1) for part in ahead))
    for row, part in ((base, lags[0]), (base + CHUNK, lags[1])):
        high = part.astype(BF16)
        high_ref[row : row + STEP, 2 * COLS : 2 * COLS + LANES] = high
        high_ref[row : row + STEP, 2 * COLS + LANES : 3 * COLS] = (part - high.astype(F32)).astype(BF16)
    back, on = with_neighbours(grads, width, odd)
    for index in range(2):
        wanted = plus(times(column(back, index), mirror), times_conjugate(column(on, index), own))
        store_split(high_ref, low_ref, base, COLS + LANES * index, wanted)


def fold(quarters):
    one, two, three, four = quarters
    between, both = HALF_ROOT * (two - four), HALF_ROOT * (two + four)
    return [one + three, two + four, one - three, two - four, one + between, -three - both, one - between, both - three]


def unfold(parts):
    between, both = HALF_ROOT * (parts[4] - parts[6]), HALF_ROOT * (parts[5] - parts[7])
    one, two = parts[0] + parts[2], parts[1] + parts[3]
    three, four = parts[0] - parts[2], parts[1] - parts[3]
    return [
        one + (parts[4] + parts[6]),
        two + (between - both),
        three - (parts[5] + parts[7]),
        four - (between + both),
    ]


def store_folded(high_ref, low_ref, row, lane, quarters):
    rows, lanes = quarters[0].shape
    for index, part in enumerate(fold(quarters)):
        start = CHUNK * index + row
        high = part.astype(BF16)
        high_ref[start : start + rows, lane : lane + lanes] = high
        low_ref[start : start + rows, lane : lane + lanes] = (part - high.astype(F32)).astype(BF16)


def transforms(inputs, table_refs, spectra_ref, high_ref, low_ref, classes_ref, result_ref, narrow, width):
    inputs_high, inputs_low = inputs
    forward_high, forward_low, backward_high, backward_low = table_refs
    chunks = BLOCK // CHUNK

    def rows_of(chunk):
        return slice(2 * CHUNK * chunk, 2 * CHUNK * (chunk + 1))

    def forward(chunk, start):
        rows = rows_of(chunk)
        columns = slice(start, start + COLS)
        spectra_ref[rows, columns] = (
            matmul(forward_high[rows, :], inputs_high[rows, columns])
            + matmul(forward_low[rows, :], inputs_high[rows, columns])
            + matmul(forward_high[rows, :], inputs_low[rows, columns])
        )

    def backward(chunk):
        rows = rows_of(chunk)
        for start in (COLS, 2 * COLS, 0):
            columns = slice(start, start + COLS)
            made = matmul(backward_high[rows, :], high_ref[rows, columns]) + matmul(
                backward_low[rows, :], high_ref[rows, columns]
            )
            if start < 2 * COLS:
                classes_ref[rows, columns] = made + matmul(backward_high[rows, :], low_ref[rows, columns])
            else:
                classes_ref[rows, start : start + LANES] = made[:, :LANES] + made[:, LANES:]

    for start in (2 * COLS, 0, COLS):
        for chunk in range(chunks):
            forward(chunk, start)
    for chunk in range(chunks):
        for base in range(2 * CHUNK * chunk, 2 * CHUNK * chunk + CHUNK, STEP):
            spectra_step(spectra_ref, high_ref, low_ref, narrow, width, base)
        backward(chunk)
    for lane in (COLS, COLS + LANES, 2 * COLS, 0, LANES):
        lanes = slice(lane, lane + LANES)
        for row in range(0, CHUNK, 32):
            parts = [classes_ref[CHUNK * index + row : CHUNK * index + row + 32, lanes] for index in range(8)]
            for quarter, part in enumerate(unfold(parts)):
                result_ref[CHUNK * quarter + row : CHUNK * quarter + row + 32, lanes] = part


def column_sum(total, narrow):
    shift = LANES // 2
    while shift >= narrow:
        total = total + pltpu.roll(total, shift, 1)
        shift //= 2
    return total


def letter_sums(values_grad, choice, belongs, narrow):
    high = values_grad.astype(BF16)
    low = (values_grad - high.astype(F32)).astype(BF16)
    sums = jnp.where(belongs, matmul(choice, high) + matmul(choice, low), 0.0)
    groups = sums.shape[0] // 4
    rows = [jnp.sum(sums[groups * a : groups * a + groups], axis=0, keepdims=True) for a in range(4)]
    total = jnp.concatenate(rows, axis=0)
    return column_sum(total[:, :LANES] + total[:, LANES:], narrow)


PLACES = [(u, s) for u in range(2) for s in range(4)]


def unpack_block(receive_ref, place, high_ref, low_ref, lanes):
    shift = owner_shift()
    for u in range(2):
        stretches = []
        for s in range(4):
            chunks = [
                receive_ref[16 * d + 4 * (2 * u + j) + s, place : place + 32, :].astype(F32)
                for j in range(2)
                for d in range(2)
            ]
            stretches.append(collect(chunks, shift))
        for q in range(4):
            store_folded(high_ref, low_ref, 32 * q, lanes + 128 * u, [rows[q] for rows in stretches])


def put(send_ref, index, pair, rows):
    start = CHUNK_ROWS * index + 2 * pair
    send_ref[start : start + rows.shape[0], :] = rows.astype(BF16)


def take(receive_ref, index, pair, count):
    return receive_ref[index, pair : pair + count].reshape(2 * count, LANES).astype(F32)


def pack_block(result_ref, lanes, send_ref, pair):
    shift = owner_shift()
    for u, s in PLACES:
        rows = [
            result_ref[128 * s + 32 * q : 128 * s + 32 * q + 32, lanes + 128 * u : lanes + 128 * u + 128]
            for q in range(4)
        ]
        for group, chunk in enumerate(spread(rows, shift)):
            j, d = group // 2, group % 2
            put(send_ref, 16 * d + 4 * (2 * u + j) + s, pair, chunk)


def unpack_taps(tails, high_ref, low_ref):
    row, lane = iota((128, 256), 0), iota((1, 256), 1)
    spot = (lane & 31) ^ ((lane >> 7) << 4)
    quarters = []
    for d in range(2):
        tail = tails[16 * d : 16 * d + 16].reshape(128, 128).astype(BF16)
        for k in range(2):
            quarters.append(matmul(tail, jnp.where(row == 32 * k + spot, 1.0, 0.0).astype(BF16)))
    store_folded(high_ref, low_ref, 0, 512, quarters)


def pack_tails(norming, tails, result_ref, send_ref):
    quarter = ((iota((128, 128), 1) >> 5) - lax.axis_index("seq")) & 3
    sums = column_sum(result_ref[:, 512:640], 32)
    lags = sums[0:128]
    for k in range(1, 4):
        lags = jnp.where(quarter == k, sums[128 * k : 128 * k + 128], lags)
    lags = lags * norming
    for index in range(16):
        put(send_ref, index, 32, lags[8 * index : 8 * index + 8])
        put(send_ref, 16 + index, 32, lags[8 * index : 8 * index + 8])
    line, source = iota((32, 128), 1), iota((32, 128), 0)
    letters = jnp.where(line < 64, pltpu.roll(tails[:, 0, :], 64, 1), tails[:, 1, :])
    choice = []
    for a in range(4):
        chosen = jnp.where(letters == float(a), 1.0, 0.0)
        choice.append(jnp.concatenate([jnp.where((source & 3) == s, chosen, 0.0) for s in range(4)], axis=1))
    choice = jnp.concatenate(choice, axis=0).astype(BF16)
    source = iota((128, 256), 0) & 31
    belongs = (((source >> 2) & 3) * 2 + (source >> 4)) == (iota((128, 256), 1) >> 5)
    sums = letter_sums(result_ref[:, 256:512], choice, belongs, 32) * norming
    sums = choose([sums[a : a + 1] for a in range(4)], 0, owner_shift())
    high = sums.astype(BF16).astype(F32)
    tile = jnp.concatenate([high, sums - high], axis=0)
    for index in range(32):
        put(send_ref, index, 36, tile)


def middle_kernel(
    norming, receive_ref, fh_ref, fl_ref, bh_ref, bl_ref, send_ref,
    inputs_high_ref, inputs_low_ref, spectra_ref, high_ref, low_ref, classes_ref, result_ref,
):
    tails = receive_ref[:, 64:72, :].astype(F32)
    unpack_taps(tails, inputs_high_ref, inputs_low_ref)
    unpack_block(receive_ref, 0, inputs_high_ref, inputs_low_ref, 0)
    unpack_block(receive_ref, 32, inputs_high_ref, inputs_low_ref, 256)
    transforms(
        (inputs_high_ref, inputs_low_ref), (fh_ref, fl_ref, bh_ref, bl_ref),
        spectra_ref, high_ref, low_ref, classes_ref, result_ref, 32, 64,
    )
    pack_tails(norming, tails, result_ref, send_ref)
    pack_block(result_ref, 256, send_ref, 16)
    pack_block(result_ref, 0, send_ref, 0)


def received_columns(receive_ref, pair, back):
    shift = stretch_shift()
    result = []
    for u in range(4):
        columns = []
        for m in (2 * u, 2 * u + 1):
            chunks = [take(receive_ref, 4 * m + d, pair, 16) for d in range(4)]
            columns.append(jnp.concatenate(collect(chunks, shift), axis=0).astype(BF16))
        result.append(matmul(jnp.concatenate(columns, axis=1), back))
    return result


def places_of(u):
    return ((slice(128 * u, 128 * u + 128), slice(0, 128)), (slice(896 - 128 * u, 1024 - 128 * u), slice(128, 256)))


def finish_kernel(receive_ref, gate_ref, upstream_ref, out_ref, hidden_ref, gated_ref, filter_ref, embedding_ref):
    back = return_channels()
    for u in range(4):
        columns = []
        for m in (2 * u, 2 * u + 1):
            columns.append(jnp.concatenate(collect([take(receive_ref, 4 * m + d, 32, 4) for d in range(4)], 0), axis=0))
        done = matmul(jnp.concatenate(columns, axis=1).astype(BF16), back)
        for there, here in places_of(u):
            filter_ref[:, :, there] = done[:, here].reshape(4, 8, 128)
    sums = collect(
        [jnp.concatenate([take(receive_ref, 4 * m + d, 36, 1) for m in range(8)], axis=0) for d in range(4)], 0
    )
    rows = []
    for term in range(2):
        for u in range(4):
            for total in sums:
                first, second = total[4 * u + term : 4 * u + term + 1], total[4 * u + 2 + term : 4 * u + 3 + term]
                rows.append(jnp.concatenate([first, second], axis=1))
    done = matmul(jnp.concatenate(rows, axis=0).astype(BF16), back)
    done = done[0:16] + done[16:32]
    for u in range(4):
        for there, here in places_of(u):
            embedding_ref[:, there] = done[4 * u : 4 * u + 4, here]
    for u, field in enumerate(received_columns(receive_ref, 0, back)):
        for there, here in places_of(u):
            out_ref[0, :, there] = (gate_ref[0, :, there].astype(F32) * field[:, here]).astype(BF16)
            gated_ref[0, :, there] = (upstream_ref[0, :, there].astype(F32) * field[:, here]).astype(BF16)
    for u, rows in enumerate(received_columns(receive_ref, 16, back)):
        for there, here in places_of(u):
            hidden_ref[0, :, there] = rows[:, here].astype(BF16)


WORK = [
    pltpu.VMEM((2 * BLOCK, 3 * COLS), BF16),
    pltpu.VMEM((2 * BLOCK, 3 * COLS), BF16),
    pltpu.VMEM((2 * BLOCK, 3 * COLS), F32),
    pltpu.VMEM((2 * BLOCK, 3 * COLS), BF16),
    pltpu.VMEM((2 * BLOCK, 2 * COLS), BF16),
    pltpu.VMEM((2 * BLOCK, 2 * COLS + LANES), F32),
    pltpu.VMEM((BLOCK, 2 * COLS + LANES), F32),
]
VM = pl.BlockSpec(memory_space=pltpu.VMEM)
HBM = pl.BlockSpec(memory_space=pltpu.HBM)


def shape_of(*dims, dtype=BF16):
    return jax.ShapeDtypeStruct(dims, dtype)


def call(kernel, specs, shapes, scratch=(), mebibytes=32):
    return pl.pallas_call(
        kernel,
        in_specs=specs,
        out_shape=shapes,
        scratch_shapes=scratch,
        compiler_params=pltpu.CompilerParams(vmem_limit_bytes=mebibytes * 1024 * 1024),
    )


def in_hbm(array):
    return pltpu.with_memory_space_constraint(array, pltpu.HBM)


def exchange(array):
    return lax.all_to_all(array, ("dp", "seq"), 0, 0, tiled=True)


def packed_device(hidden, letters, gate_input, cotangent, embedding, filter_taps, norming):
    stretch = pltpu.VMEM(hidden.shape, BF16)
    sent = call(
        pack_kernel,
        [HBM] * 6,
        shape_of(32, 72, 128),
        [
            stretch,
            pltpu.VMEM(letters.shape, jnp.int32),
            stretch,
            stretch,
            pltpu.VMEM(embedding.shape, F32),
            pltpu.VMEM((2, 8, 1024), BF16),
            pltpu.SemaphoreType.DMA((6,)),
        ],
        16,
    )(*(in_hbm(array) for array in (hidden, letters, gate_input, cotangent, embedding, filter_taps)))
    here = exchange(sent)
    def kernel(*refs):
        middle_kernel(norming, *refs)

    sent = call(
        kernel,
        [VM] * 5,
        shape_of(32 * CHUNK_ROWS, LANES),
        WORK,
        24,
    )(here, *tables())
    here = exchange(sent.reshape(32, CHUNK_ROWS // 2, 2, LANES))
    shape = jax.ShapeDtypeStruct(hidden.shape, BF16)
    return call(
        finish_kernel,
        [VM] * 3,
        (shape, shape, shape, shape_of(*filter_taps.shape, dtype=F32), shape_of(*embedding.shape, dtype=F32)),
        (),
        16,
    )(here, gate_input, cotangent)


def plain_kernel(
    narrow, width, letters_ref, samples_ref, fh_ref, fl_ref, bh_ref, bl_ref, field_ref, back_ref, lags_ref, sums_ref,
    inputs_high_ref, inputs_low_ref, spectra_ref, high_ref, low_ref, classes_ref, result_ref,
):
    for lane in range(0, 3 * COLS, LANES):
        quarters = [samples_ref[row : row + CHUNK, lane : lane + LANES].astype(F32) for row in range(0, BLOCK, CHUNK)]
        store_folded(inputs_high_ref, inputs_low_ref, 0, lane, quarters)
    transforms(
        (inputs_high_ref, inputs_low_ref), (fh_ref, fl_ref, bh_ref, bl_ref),
        spectra_ref, high_ref, low_ref, classes_ref, result_ref, narrow, width,
    )
    field_ref[...] = result_ref[:, 0:COLS].astype(BF16)
    back_ref[...] = result_ref[:, COLS : 2 * COLS].astype(BF16)
    lags_ref[...] = column_sum(result_ref[:, 2 * COLS :], narrow)
    letters = letters_ref[...]
    groups = COLS // narrow
    choice = jnp.concatenate(
        [jnp.where(letters == float(a), 1.0, 0.0) for a in range(4)], axis=0
    ).astype(BF16)
    shape = (4 * groups, COLS)
    belongs = (iota(shape, 0) & (groups - 1)) == iota(shape, 1) // narrow
    sums_ref[...] = letter_sums(result_ref[:, COLS : 2 * COLS], choice, belongs, narrow)


def plain_device(hidden, letters, gate_input, cotangent, embedding, filter_taps, norming):
    axes = ("dp", "seq")
    copies, stretches = lax.axis_size("dp"), lax.axis_size("seq")
    devices = copies * stretches
    stretch, channels = hidden.shape[1], hidden.shape[2]
    narrow = channels // devices
    half = narrow // 2
    blocks = stretch * stretches // BLOCK
    low = np.arange(channels // 2).reshape(devices, half)
    order = np.concatenate([low, channels - 1 - low], axis=1).reshape(-1)
    restore = np.argsort(order)
    onehot = (letters[0][:, None] == jnp.arange(embedding.shape[0], dtype=jnp.int32)[None, :]).astype(F32)
    added = jnp.dot(onehot, embedding, precision=lax.Precision.HIGHEST)
    values = (hidden[0].astype(F32) + added).astype(BF16)
    gate_wide, upstream = gate_input[0].astype(F32), cotangent[0].astype(F32)
    field_grad = (upstream * gate_wide).astype(BF16)

    def scatter(array):
        parts = jnp.take(array, order, axis=1).reshape(stretch, devices, narrow).swapaxes(0, 1)
        parts = lax.all_to_all(parts, axes, 0, 0, tiled=True)
        parts = parts.reshape(copies, blocks, BLOCK, narrow)
        return parts.transpose(2, 1, 0, 3).reshape(BLOCK, COLS)

    def gather(columns):
        parts = columns.reshape(BLOCK, blocks, copies, narrow).transpose(2, 1, 0, 3)
        parts = parts.reshape(devices, stretch, narrow)
        parts = lax.all_to_all(parts, axes, 0, 0, tiled=True)
        return jnp.take(parts.swapaxes(0, 1).reshape(stretch, channels), restore, axis=1)

    taps = lax.all_gather(filter_taps, "seq", axis=1, tiled=True).reshape(BLOCK, channels)
    mine = lax.axis_index("dp") * stretches + lax.axis_index("seq")
    own = lax.dynamic_slice_in_dim(jnp.take(taps, order, axis=1), mine * narrow, narrow, axis=1)
    mirror = jnp.roll(own, half, axis=1)
    repeats = LANES // narrow
    samples = jnp.concatenate(
        [scatter(values), scatter(field_grad), jnp.tile(own, (1, repeats)), jnp.tile(mirror, (1, repeats))], axis=1
    )
    marks = lax.all_gather(letters[0].astype(F32), axes, tiled=True)
    marks = marks.reshape(copies, blocks, BLOCK).swapaxes(0, 1).reshape(copies * blocks, BLOCK)

    def kernel(*refs):
        plain_kernel(narrow, copies * narrow, *refs)

    field, back, lags, sums = call(
        kernel,
        [VM] * 6,
        (
            shape_of(BLOCK, COLS),
            shape_of(BLOCK, COLS),
            shape_of(BLOCK, LANES, dtype=F32),
            shape_of(embedding.shape[0], LANES, dtype=F32),
        ),
        WORK,
    )(marks, samples, *tables())
    small = jnp.concatenate([lags[:, :narrow], sums[:, :narrow]], axis=0) * norming
    small = jnp.take(lax.all_gather(small, axes, axis=1, tiled=True), restore, axis=1)
    rows = filter_taps.shape[1]
    filter_grad = lax.dynamic_slice_in_dim(
        small[:BLOCK].reshape(filter_taps.shape[0], stretch, channels), lax.axis_index("seq") * rows, rows, axis=1
    )
    field_rows, grad_rows = gather(field).astype(F32), gather(back)
    output = (gate_wide * field_rows).astype(BF16)[None]
    gate_grad = (upstream * field_rows).astype(BF16)[None]
    return output, grad_rows[None], gate_grad, filter_grad, small[BLOCK:]


def per_device(hidden, letters, gate_input, cotangent, embedding, filter_taps):
    copies, stretches = lax.axis_size("dp"), lax.axis_size("seq")
    norming = 1.0 / math.sqrt(copies * hidden.shape[0] * hidden.shape[1] * stretches)
    device = packed_device if (copies, stretches) == (2, 16) else plain_device
    return device(hidden, letters, gate_input, cotangent, embedding, filter_taps, norming)


def solution(mesh):
    return jax.shard_map(
        per_device,
        mesh=mesh,
        in_specs=(
            P("dp", "seq", None),
            P("dp", "seq"),
            P("dp", "seq", None),
            P("dp", "seq", None),
            P(),
            P(None, "seq", None),
        ),
        out_specs=(
            P("dp", "seq", None),
            P("dp", "seq", None),
            P("dp", "seq", None),
            P(None, "seq", None),
            P(),
        ),
        check_vma=False,
    )
```
